128 devices in a mesh: seq: 32 (over z, y, x_lo), samp: 4 (over x_hi, core).
Axes of the slice: x: 4 (x_hi: 2, x_lo: 2; x = x_hi * 2 + x_lo), y: 4, z: 4, core: 2. Of those that a mesh axis runs over, the one named last changes fastest.
Arguments:
- queries: bfloat16 [4, 4096, 5120], P('samp', 'seq'), may hold values from -120 to 120
- prefix_keys: bfloat16 [4096, 1024], P('seq'), may hold values from -4 to 4
- prefix_values: bfloat16 [4096, 1024], P('seq'), may hold values from -4 to 4
- suffix_keys: bfloat16 [4, 4096, 1024], P('samp', 'seq'), may hold values from -5 to 5
- suffix_values: bfloat16 [4, 4096, 1024], P('samp', 'seq'), may hold values from -4 to 4
- layout_pre: int32 [4, 32, 32], P('samp', 'seq'), may hold values 0 or 1
- layout_suf: int32 [4, 32, 32], P('samp', 'seq'), may hold values 0 or 1
- lengths: int32 [4], P('samp'), may hold values from 1 to 32
Outputs:
- attended: bfloat16 [4, 4096, 5120], P('samp', 'seq')
The draws below stay inside these ranges and needn't reach their ends.
All inputs are finite; a program needn't handle non-finite values. No bound on the sum of `layout_pre` or of `layout_suf` on one device may be relied on, other than what follows from the above.
Results may differ from the reference program's by a relative error of at most 0.004.
Values may be sent and summed in bfloat16 or wider, within the bound.
A program may use at most 128 MiB of HBM per device.

```python
import math
import jax
import jax.numpy as jnp
from jax import lax

HEADS = 40
KV_HEADS = 8
HEAD_DIM = 128
BLOCK = 128
PREFIX = 4096
SUFFIX = 4096
SAMPLES = 4
PRE_BLOCKS = 32
SUF_BLOCKS = 32


def draw_pair(key):
    shape_keys = (SAMPLES, SUFFIX, KV_HEADS * HEAD_DIM)
    base_keys = jnp.clip(jax.random.normal(jax.random.fold_in(key, 11), shape_keys, jnp.float32), -4.0, 4.0)
    base_queries = 2.5 * jnp.clip(jax.random.normal(jax.random.fold_in(key, 12), (SAMPLES, SUFFIX, HEADS * HEAD_DIM), jnp.float32), -4.0, 4.0)
    return (base_queries, base_keys)


def draw_queries(key, part):
    return draw_pair(key)[0].astype(jnp.bfloat16)


def draw_suffix_keys(key, part):
    return draw_pair(key)[1].astype(jnp.bfloat16)


def plant(array, key, least, high):
    shape = array.shape
    index_at = [jax.random.randint(jax.random.fold_in(key, axis), (), 0, shape[axis]) for axis in range(len(shape))]
    array = array.at[tuple(index_at)].set(least)
    longest = shape.index(max(shape))
    index_at[longest] = (index_at[longest] + 1) % shape[longest]
    return array.at[tuple(index_at)].set(high)


def block_scale(key, extent, cuts, smallest, high):
    factor_of, own = 1.0, jax.random.fold_in(key, 6)
    for axis_at, parts in cuts:
        heights = jnp.exp(jax.random.uniform(jax.random.fold_in(own, axis_at), (parts,), jnp.float32, smallest / len(cuts), high / len(cuts)))
        factor_of = factor_of * jnp.repeat(heights, extent[axis_at] // parts).reshape([-1 if axis == axis_at else 1 for axis in range(len(extent))])
    return factor_of


def bell_draw(own_key, extent, spread, reach, split=(), held_as=jnp.bfloat16):
    drawn = jax.random.normal(own_key, extent, jnp.float32) * spread
    if len(split) > 0:
        drawn = block_scale(own_key, extent, split, -0.22, 0.18) * drawn
    return jnp.clip(drawn, min=-reach, max=reach).astype(held_as)


def setup_inputs(seed: int = 0) -> dict:
    streams_of = jax.random.split(jax.random.key(seed), 9)
    return {
        "queries": draw_queries(jax.random.fold_in(streams_of[8], 71), 0),
        "prefix_keys": bell_draw(streams_of[1], (PREFIX, KV_HEADS * HEAD_DIM), 1.0, 4.0, ((0, 32),)),
        "prefix_values": bell_draw(streams_of[2], (PREFIX, KV_HEADS * HEAD_DIM), 1.0, 4.0, ((0, 32),)),
        "suffix_keys": draw_suffix_keys(jax.random.fold_in(streams_of[8], 71), 0),
        "suffix_values": bell_draw(streams_of[4], (SAMPLES, SUFFIX, KV_HEADS * HEAD_DIM), 1.0, 4.0, ((0, 4), (1, 32))),
        "layout_pre": plant((jax.random.randint(streams_of[5], (SAMPLES, SUF_BLOCKS, PRE_BLOCKS), 0, 3) < 1).astype(jnp.int32), jax.random.fold_in(streams_of[5], 1), 0, 1),
        "layout_suf": plant((jax.random.randint(streams_of[6], (SAMPLES, SUF_BLOCKS, SUF_BLOCKS), 0, 2) < 1).astype(jnp.int32), jax.random.fold_in(streams_of[6], 1), 0, 1),
        "lengths": plant(jax.random.randint(streams_of[7], (SAMPLES,), 1, SUF_BLOCKS + 1), jax.random.fold_in(streams_of[7], 1), 1, SUF_BLOCKS).astype(jnp.int32),
    }


masked_value = -1e+30

def reference(queries, prefix_keys, prefix_values, suffix_keys, suffix_values, layout_pre, layout_suf, lengths):
    group_size = HEADS // KV_HEADS
    score_scale = 1.0 / math.sqrt(HEAD_DIM)
    prefix_key_rows = prefix_keys.astype(jnp.float32).reshape(PREFIX, KV_HEADS, HEAD_DIM)
    prefix_value_rows = prefix_values.astype(jnp.float32).reshape(PREFIX, KV_HEADS, HEAD_DIM)
    prefix_block = jnp.arange(PREFIX, dtype=jnp.int32) // BLOCK
    suffix_position = jnp.arange(SUFFIX, dtype=jnp.int32)
    suffix_block = suffix_position // BLOCK

    def one_block(flat_index):
        sample = flat_index // SUF_BLOCKS
        block_index = flat_index % SUF_BLOCKS
        query_rows = lax.dynamic_slice_in_dim(queries[sample], (block_index * BLOCK).astype(jnp.int32), BLOCK, 0)
        query_grid = query_rows.astype(jnp.float32).reshape(BLOCK, KV_HEADS, group_size, HEAD_DIM)
        key_rows = jnp.concatenate([prefix_key_rows, suffix_keys[sample].astype(jnp.float32).reshape(SUFFIX, KV_HEADS, HEAD_DIM)], axis=0)
        value_rows = jnp.concatenate([prefix_value_rows, suffix_values[sample].astype(jnp.float32).reshape(SUFFIX, KV_HEADS, HEAD_DIM)], axis=0)
        scores = jnp.einsum('qgjd,lgd->gjql', query_grid, key_rows) * score_scale
        prefix_seen = layout_pre[sample, block_index][prefix_block] > 0
        query_position = block_index * BLOCK + jnp.arange(BLOCK, dtype=jnp.int32)
        suffix_seen = ((suffix_block == block_index) | (layout_suf[sample, block_index][suffix_block] > 0))[None, :]
        suffix_seen = suffix_seen & (suffix_position[None, :] <= query_position[:, None])
        key_mask = jnp.concatenate([jnp.broadcast_to(prefix_seen[None, :], (BLOCK, PREFIX)), suffix_seen], axis=1)
        row_max = lax.optimization_barrier(jnp.max(jnp.where(key_mask, scores, masked_value), axis=-1, keepdims=True))
        weights = jnp.where(key_mask, jnp.exp(scores - row_max), 0.0)
        run_total = lax.optimization_barrier(jnp.sum(weights, axis=-1))
        rounded = lax.optimization_barrier(weights.astype(jnp.bfloat16)).astype(jnp.float32)
        mixed = jnp.einsum('gjql,lgd->qgjd', rounded, value_rows) / jnp.transpose(run_total, (2, 0, 1))[..., None]
        is_live = block_index < lengths[sample]
        return jnp.where(is_live, mixed.reshape(BLOCK, HEADS * HEAD_DIM), 0.0).astype(jnp.bfloat16)
    blocks = lax.map(one_block, jnp.arange(SAMPLES * SUF_BLOCKS, dtype=jnp.int32))
    return blocks.reshape(SAMPLES, SUFFIX, HEADS * HEAD_DIM)
```

```python
import math

import jax
import jax.numpy as jnp
from jax import lax
from jax.experimental import pallas as pl
from jax.experimental.pallas import tpu as pltpu
from jax.sharding import PartitionSpec as P

HEADS = 40
KV_HEADS = 8
HEAD_DIM = 128
BLOCK = 128
GROUP = HEADS // KV_HEADS
WIDE = GROUP * HEAD_DIM
CHUNK = 4
UNITS = 8
MASKED = -1e30
MESH = pl.DeviceIdType.MESH
BF16 = jnp.bfloat16

STEPS = ((0, 0), (0, 1), (1, 0), (3, 0), (1, 1), (3, 1), (2, 0), (2, 1))


class Place:
    def __init__(self):
        seq = lax.axis_index("seq")
        samp = lax.axis_index("samp")
        self.z = seq // 8
        self.y = lax.rem(seq // 2, 4)
        self.x = lax.rem(seq, 2)
        self.half = samp // 2
        self.core = lax.rem(samp, 2)
        self.member = self.z * 2 + self.x

    def device(self, dz=0, dy=0, dx=0, dc=0):
        z = lax.rem(self.z + dz, 4)
        y = lax.rem(self.y + dy, 4)
        x = lax.rem(self.x + dx, 2)
        core = lax.rem(self.core + dc, 2)
        return ((z * 4 + y) * 2 + x, self.half * 2 + core)

    def member_at(self, dz, dx):
        return lax.rem(self.z + dz, 4) * 2 + lax.rem(self.x + dx, 2)


def columns(member, width):
    return pl.ds(pl.multiple_of(member * width, width), width)


def meet(partners):
    barrier = pltpu.get_barrier_semaphore()
    for partner in partners:
        pl.semaphore_signal(barrier, inc=1, device_id=partner, device_id_type=MESH)
    pl.semaphore_wait(barrier, len(partners))


def plane_partners(at):
    partners = []
    for dz, dx in STEPS[1:]:
        partners.append(at.device(dz=dz, dx=dx))
        if dx:
            partners.append(at.device(dz=dz, dx=dx, dc=1))
    return partners


def gather_kernel(
    q_ref, pk_ref, pv_ref, sk_ref, sv_ref, lay_ref, kv_ref, qall_ref, layall_ref,
    kv_vm, pre_vm, q_vm, lay_vm, local_sem,
    a_suf_s, a_suf_r, a_pre_s, a_pre_r, a_q_s, a_q_r, a_lay_s, a_lay_r,
    y_suf_s, y_suf_r, y_pre_s, y_pre_r,
    c_suf_s, c_suf_r, c_pre_s, c_pre_r,
):
    at = Place()
    half_rows = BLOCK // 2
    mine = pl.ds(pl.multiple_of(at.core * half_rows, half_rows), half_rows)
    other = pl.ds(pl.multiple_of((1 - at.core) * half_rows, half_rows), half_rows)
    up, down = at.device(dy=1), at.device(dy=3)
    twin = at.device(dc=1)
    meet(plane_partners(at) + [up, down, twin])

    def send(src, dst, send_sem, recv_sem, device):
        pltpu.make_async_remote_copy(
            src_ref=src, dst_ref=dst, send_sem=send_sem, recv_sem=recv_sem, device_id=device, device_id_type=MESH
        ).start()

    def suf_at(dy, member):
        return 32 + lax.rem(at.y + dy, 4) * 8 + member

    def pre_at(dy, member):
        return lax.rem(at.y + dy, 4) * 8 + member

    own_columns = columns(at.member, HEAD_DIM)
    own_k, own_v = sk_ref.at[:, own_columns], sv_ref.at[:, own_columns]
    own_pk, own_pv = pk_ref.at[mine, own_columns], pv_ref.at[mine, own_columns]
    suf_here, pre_here = suf_at(0, at.member), pre_at(0, at.member)

    for t in range(1, UNITS):
        dz, dx = STEPS[t]
        device = at.device(dz=dz, dx=dx)
        there = columns(at.member_at(dz, dx), HEAD_DIM)
        send(sk_ref.at[:, there], kv_ref.at[suf_here, 0], a_suf_s.at[t], a_suf_r.at[t], device)
        send(sv_ref.at[:, there], kv_ref.at[suf_here, 1], a_suf_s.at[t], a_suf_r.at[t], device)
        send(pk_ref.at[mine, there], kv_ref.at[pre_here, 0, mine], a_pre_s.at[t], a_pre_r.at[t], device)
        send(pv_ref.at[mine, there], kv_ref.at[pre_here, 1, mine], a_pre_s.at[t], a_pre_r.at[t], device)
    for way, device in ((0, up), (1, down)):
        send(own_k, kv_ref.at[suf_here, 0], y_suf_s.at[way, 0], y_suf_r.at[way, 0], device)
        send(own_v, kv_ref.at[suf_here, 1], y_suf_s.at[way, 0], y_suf_r.at[way, 0], device)
        send(own_pk, kv_ref.at[pre_here, 0, mine], y_pre_s.at[way, 0], y_pre_r.at[way, 0], device)
        send(own_pv, kv_ref.at[pre_here, 1, mine], y_pre_s.at[way, 0], y_pre_r.at[way, 0], device)
    send(own_k, kv_ref.at[suf_here + 32, 0], c_suf_s.at[0, 0], c_suf_r.at[0, 0], twin)
    send(own_v, kv_ref.at[suf_here + 32, 1], c_suf_s.at[0, 0], c_suf_r.at[0, 0], twin)
    send(own_pk, kv_ref.at[pre_here, 0, mine], c_pre_s.at[0, 0], c_pre_r.at[0, 0], twin)
    send(own_pv, kv_ref.at[pre_here, 1, mine], c_pre_s.at[0, 0], c_pre_r.at[0, 0], twin)
    for t in range(1, UNITS):
        dz, dx = STEPS[t]
        device = at.device(dz=dz, dx=dx, dc=dx)
        there = columns(at.member_at(dz, dx), WIDE)
        send(lay_ref, layall_ref.at[at.z * 2 + dx], a_lay_s.at[t], a_lay_r.at[t], device)
        send(q_ref.at[:, there], qall_ref.at[at.z * 2 + dx], a_q_s.at[t], a_q_r.at[t], device)

    q_columns = columns(at.member, WIDE)
    incoming = [
        pltpu.make_async_copy(own_k, kv_vm.at[0], local_sem.at[0]),
        pltpu.make_async_copy(own_v, kv_vm.at[1], local_sem.at[1]),
        pltpu.make_async_copy(own_pk, pre_vm.at[0], local_sem.at[2]),
        pltpu.make_async_copy(own_pv, pre_vm.at[1], local_sem.at[3]),
        pltpu.make_async_copy(q_ref.at[:, q_columns], q_vm, local_sem.at[4]),
        pltpu.make_async_copy(lay_ref, lay_vm, local_sem.at[5]),
    ]
    outgoing = [
        pltpu.make_async_copy(kv_vm.at[0], kv_ref.at[suf_here, 0], local_sem.at[6]),
        pltpu.make_async_copy(kv_vm.at[1], kv_ref.at[suf_here, 1], local_sem.at[7]),
        pltpu.make_async_copy(pre_vm.at[0], kv_ref.at[pre_here, 0, mine], local_sem.at[8]),
        pltpu.make_async_copy(pre_vm.at[1], kv_ref.at[pre_here, 1, mine], local_sem.at[9]),
        pltpu.make_async_copy(q_vm, qall_ref.at[at.z * 2], local_sem.at[10]),
        pltpu.make_async_copy(lay_vm, layall_ref.at[at.z * 2], local_sem.at[11]),
    ]
    for copy in incoming:
        copy.start()
    for first, second in zip(incoming, outgoing):
        first.wait()
        second.start()

    def suf_block(dy, member):
        return kv_ref.at[suf_at(dy, member)]

    def pre_block(dy, member, rows=mine):
        return kv_ref.at[pre_at(dy, member), :, rows]

    def arrived(block, sem):
        pltpu.make_async_copy(block, block, sem).wait()

    def source(t):
        dz, dx = STEPS[t]
        return at.member_at(4 - dz, dx)

    def to_twin(dy, t):
        member = source(t)
        place = suf_at(dy, member)
        send(kv_ref.at[place], kv_ref.at[place + 32], c_suf_s.at[dy, t], c_suf_r.at[dy, t], twin)
        block = pre_block(dy, member)
        send(block, block, c_pre_s.at[dy, t], c_pre_r.at[dy, t], twin)

    def from_plane(t):
        member = source(t)
        suf, pre = suf_block(0, member), pre_block(0, member)
        arrived(suf, a_suf_r.at[t])
        for way, device in ((0, up), (1, down)):
            send(suf, suf, y_suf_s.at[way, t], y_suf_r.at[way, t], device)
        arrived(pre, a_pre_r.at[t])
        for way, device in ((0, up), (1, down)):
            send(pre, pre, y_pre_s.at[way, t], y_pre_r.at[way, t], device)
        to_twin(0, t)

    def from_sides(t):
        member = source(t)
        for way, dy, onward in ((0, 3, up), (1, 1, down)):
            suf, pre = suf_block(dy, member), pre_block(dy, member)
            arrived(suf, y_suf_r.at[way, t])
            relays = (t % 2) == way
            if relays:
                send(suf, suf, y_suf_s.at[2, t], y_suf_r.at[2, t], onward)
            arrived(pre, y_pre_r.at[way, t])
            if relays:
                send(pre, pre, y_pre_s.at[2, t], y_pre_r.at[2, t], onward)
            to_twin(dy, t)

    def from_far(t):
        member = source(t)
        arrived(suf_block(2, member), y_suf_r.at[2, t])
        arrived(pre_block(2, member), y_pre_r.at[2, t])
        to_twin(2, t)

    for t in range(UNITS + 2):
        if 1 <= t < UNITS:
            from_plane(t)
        if 0 <= t - 1 < UNITS:
            from_sides(t - 1)
        if 0 <= t - 2 < UNITS:
            from_far(t - 2)

    for t in range(UNITS):
        member = source(t)
        for dy in range(4):
            arrived(kv_ref.at[suf_at(dy, member) + 32], c_suf_r.at[dy, t])
            arrived(pre_block(dy, member, other), c_pre_r.at[dy, t])
    for t in range(1, UNITS):
        dz, dx = STEPS[t]
        slot = lax.rem(at.z + 4 - dz, 4) * 2 + dx
        arrived(qall_ref.at[slot], a_q_r.at[t])
        arrived(layall_ref.at[slot], a_lay_r.at[t])
    suf, pre = suf_block(0, at.member), pre_block(0, at.member)
    for t in range(UNITS):
        if t:
            arrived(suf, a_suf_s.at[t])
            arrived(pre, a_pre_s.at[t])
            arrived(qall_ref.at[at.z * 2], a_q_s.at[t])
            arrived(layall_ref.at[at.z * 2], a_lay_s.at[t])
        for way in range(3):
            arrived(suf, y_suf_s.at[way, t])
            arrived(pre, y_pre_s.at[way, t])
        for dy in range(4):
            arrived(suf, c_suf_s.at[dy, t])
            arrived(pre, c_pre_s.at[dy, t])
    for copy in outgoing:
        copy.wait()


def gather(queries, prefix_keys, prefix_values, suffix_keys, suffix_values, layout):
    dma = pltpu.SemaphoreType.DMA
    anywhere = pl.BlockSpec(memory_space=pl.ANY)
    return pl.pallas_call(
        gather_kernel,
        name="gather",
        out_shape=(
            jax.ShapeDtypeStruct((96, 2, BLOCK, HEAD_DIM), BF16),
            jax.ShapeDtypeStruct((UNITS, BLOCK, WIDE), BF16),
            jax.ShapeDtypeStruct((UNITS, 1, 128), jnp.int32),
        ),
        in_specs=[anywhere] * 6,
        out_specs=(anywhere,) * 3,
        scratch_shapes=[
            pltpu.VMEM((2, BLOCK, HEAD_DIM), BF16),
            pltpu.VMEM((2, BLOCK // 2, HEAD_DIM), BF16),
            pltpu.VMEM((BLOCK, WIDE), BF16),
            pltpu.VMEM((1, 128), jnp.int32),
            dma((12,)),
        ]
        + [dma((UNITS,))] * 8
        + [dma((3, UNITS))] * 4
        + [dma((4, UNITS))] * 4,
        compiler_params=pltpu.CompilerParams(collective_id=0, has_side_effects=True),
    )(queries, prefix_keys, prefix_values, suffix_keys, suffix_values, layout)


def attend_kernel(lay_ref, q_ref, kv_ref, o_ref, table, m_ref, l_ref, acc_ref):
    unit = pl.program_id(0)
    at = Place()
    flip = lax.rem(unit, 2)
    block = ((unit // 2) * 4 + at.y) * 2 + lax.rem(at.x + flip, 2)
    live = block < lay_ref[unit, 64]
    factor = math.log2(math.e) / math.sqrt(HEAD_DIM)

    def place_of(j):
        return ((j // 2) % 4) * 8 + (j // 8) * 2 + j % 2

    @pl.when(jnp.logical_not(live))
    def _():
        o_ref[...] = jnp.zeros_like(o_ref)

    @pl.when(live)
    def _():
        count = jnp.int32(0)
        for j in range(32):
            table[count] = jnp.int32(place_of(j))
            count = count + jnp.where(lay_ref[unit, j] > 0, 1, 0)
        suffix_base = 32 + 32 * flip
        for j in range(32):
            table[count] = suffix_base + place_of(j)
            count = count + jnp.where((lay_ref[unit, 32 + j] > 0) & (j < block), 1, 0)
        diagonal = suffix_base + lax.rem(block // 2, 4) * 8 + (block // 8) * 2 + lax.rem(block, 2)
        spare = lax.rem(count, CHUNK)
        q = jnp.concatenate([q_ref[0, :, g * HEAD_DIM:(g + 1) * HEAD_DIM] for g in range(GROUP)], axis=0)

        def scores_of(places):
            k = jnp.concatenate([kv_ref[p, 0] for p in places], axis=0)
            return lax.dot_general(q, k, (((1,), (1,)), ((), ())), preferred_element_type=jnp.float32)

        def product(weights, places):
            v = jnp.concatenate([kv_ref[p, 1] for p in places], axis=0)
            return lax.dot_general(
                weights.astype(BF16), v, (((1,), (0,)), ((), ())), preferred_element_type=jnp.float32
            )

        def spread(column, width):
            return jnp.broadcast_to(column, (column.shape[0], width))

        wide = CHUNK * BLOCK
        places = [diagonal]
        for s in range(CHUNK - 1):
            places.append(jnp.where(s < spare, table[s], diagonal))
        s = scores_of(places)
        row = lax.broadcasted_iota(jnp.int32, s.shape, 0) % BLOCK
        col = lax.broadcasted_iota(jnp.int32, s.shape, 1)
        last = jnp.where(col < BLOCK, row, (spare + 1) * BLOCK - 1)
        s = jnp.where(col <= last, s, MASKED)
        top = jnp.max(s, axis=1, keepdims=True)
        weights = jnp.exp2((s - top) * factor)
        m_ref[...] = spread(top, 128)
        l_ref[...] = spread(jnp.sum(weights, axis=1, keepdims=True), 128)
        acc_ref[...] = product(weights, places)

        @pl.loop(0, count // CHUNK)
        def _(step):
            first = spare + step * CHUNK
            places = [table[first + s] for s in range(CHUNK)]
            s = scores_of(places)
            old = m_ref[...]
            new = jnp.maximum(old, spread(jnp.max(s, axis=1, keepdims=True), 128))
            scale = jnp.exp2((old - new) * factor)
            weights = jnp.exp2((s - jnp.concatenate([new] * CHUNK, axis=1)) * factor)
            m_ref[...] = new
            l_ref[...] = l_ref[...] * scale + spread(jnp.sum(weights, axis=1, keepdims=True), 128)
            acc_ref[...] = acc_ref[...] * scale + product(weights, places)

        out = (acc_ref[...] / l_ref[...]).astype(BF16)
        for g in range(GROUP):
            o_ref[0, :, g * HEAD_DIM:(g + 1) * HEAD_DIM] = out[g * BLOCK:(g + 1) * BLOCK]


def attend(layout, queries, kv):
    rows = GROUP * BLOCK
    return pl.pallas_call(
        attend_kernel,
        name="attend",
        grid=(UNITS,),
        out_shape=jax.ShapeDtypeStruct((UNITS, BLOCK, WIDE), BF16),
        in_specs=[
            pl.BlockSpec(memory_space=pltpu.SMEM),
            pl.BlockSpec((1, BLOCK, WIDE), lambda u: (u, 0, 0)),
            pl.BlockSpec((96, 2, BLOCK, HEAD_DIM), lambda u: (0, 0, 0, 0), pipeline_mode=pl.Buffered(1)),
        ],
        out_specs=pl.BlockSpec((1, BLOCK, WIDE), lambda u: (u, 0, 0)),
        scratch_shapes=[
            pltpu.SMEM((72,), jnp.int32),
            pltpu.VMEM((rows, 128), jnp.float32),
            pltpu.VMEM((rows, 128), jnp.float32),
            pltpu.VMEM((rows, HEAD_DIM), jnp.float32),
        ],
        compiler_params=pltpu.CompilerParams(dimension_semantics=("arbitrary",)),
    )(layout, queries, kv)


def spread_kernel(part_ref, out_ref, vm, local_sem, send_sem, recv_sem):
    at = Place()
    partners = [at.device(dz=dz, dx=dx, dc=dx) for dz, dx in STEPS[1:]]
    meet(partners)
    here = columns(at.member, WIDE)
    for t in range(1, UNITS):
        dz, dx = STEPS[t]
        pltpu.make_async_remote_copy(
            src_ref=part_ref.at[lax.rem(at.z + dz, 4) * 2 + dx],
            dst_ref=out_ref.at[:, here],
            send_sem=send_sem.at[t],
            recv_sem=recv_sem.at[t],
            device_id=partners[t - 1],
            device_id_type=MESH,
        ).start()
    inward = pltpu.make_async_copy(part_ref.at[at.z * 2], vm, local_sem.at[0])
    outward = pltpu.make_async_copy(vm, out_ref.at[:, here], local_sem.at[1])
    inward.start()
    inward.wait()
    outward.start()
    for t in range(1, UNITS):
        dz, dx = STEPS[t]
        there = out_ref.at[:, columns(at.member_at(4 - dz, dx), WIDE)]
        pltpu.make_async_copy(there, there, recv_sem.at[t]).wait()
        gone = part_ref.at[lax.rem(at.z + dz, 4) * 2 + dx]
        pltpu.make_async_copy(gone, gone, send_sem.at[t]).wait()
    outward.wait()


def spread(parts):
    dma = pltpu.SemaphoreType.DMA
    anywhere = pl.BlockSpec(memory_space=pl.ANY)
    return pl.pallas_call(
        spread_kernel,
        name="spread",
        out_shape=jax.ShapeDtypeStruct((BLOCK, HEADS * HEAD_DIM), BF16),
        in_specs=[anywhere],
        out_specs=anywhere,
        scratch_shapes=[pltpu.VMEM((BLOCK, WIDE), BF16), dma((2,)), dma((UNITS,)), dma((UNITS,))],
        compiler_params=pltpu.CompilerParams(collective_id=1, has_side_effects=True),
    )(parts)


def shards(
    queries, prefix_keys, prefix_values, suffix_keys, suffix_values, layout_pre, layout_suf, lengths
):
    layout = jnp.concatenate(
        [layout_pre[0], layout_suf[0], jnp.broadcast_to(lengths[:, None], (1, 64))], axis=1
    )
    kv, q_all, layouts = gather(
        queries[0], prefix_keys, prefix_values, suffix_keys[0], suffix_values[0], layout
    )
    parts = attend(layouts[:, 0], q_all, kv)
    return spread(parts)[None]


def solution(mesh):
    return jax.shard_map(
        shards,
        mesh=mesh,
        in_specs=(
            P("samp", "seq", None),
            P("seq", None),
            P("seq", None),
            P("samp", "seq", None),
            P("samp", "seq", None),
            P("samp", "seq", None),
            P("samp", "seq", None),
            P("samp"),
        ),
        out_specs=P("samp", "seq", None),
        check_vma=False,
    )
```

```python
import math

import jax
import jax.numpy as jnp
from jax import lax
from jax.experimental import pallas as pl
from jax.experimental.pallas import tpu as pltpu
from jax.sharding import PartitionSpec as P

HEADS = 40
KV_HEADS = 8
HEAD_DIM = 128
BLOCK = 128
GROUP = HEADS // KV_HEADS
WIDE = GROUP * HEAD_DIM
CHUNK = 4
UNITS = 8
MASKED = -1e30
MESH = pl.DeviceIdType.MESH
BF16 = jnp.bfloat16

STEPS = ((0, 0), (0, 1), (1, 0), (3, 0), (1, 1), (3, 1), (2, 0), (2, 1))


class Place:
    def __init__(self):
        seq = lax.axis_index("seq")
        samp = lax.axis_index("samp")
        self.z = seq // 8
        self.y = lax.rem(seq // 2, 4)
        self.x = lax.rem(seq, 2)
        self.half = samp // 2
        self.core = lax.rem(samp, 2)
        self.member = self.z * 2 + self.x

    def device(self, dz=0, dy=0, dx=0, dc=0):
        z = lax.rem(self.z + dz, 4)
        y = lax.rem(self.y + dy, 4)
        x = lax.rem(self.x + dx, 2)
        core = lax.rem(self.core + dc, 2)
        return ((z * 4 + y) * 2 + x, self.half * 2 + core)

    def member_at(self, dz, dx):
        return lax.rem(self.z + dz, 4) * 2 + lax.rem(self.x + dx, 2)


def columns(member, width):
    return pl.ds(pl.multiple_of(member * width, width), width)


def meet(partners):
    barrier = pltpu.get_barrier_semaphore()
    for partner in partners:
        pl.semaphore_signal(barrier, inc=1, device_id=partner, device_id_type=MESH)
    pl.semaphore_wait(barrier, len(partners))


def plane_partners(at):
    partners = []
    for dz, dx in STEPS[1:]:
        partners.append(at.device(dz=dz, dx=dx))
        if dx:
            partners.append(at.device(dz=dz, dx=dx, dc=1))
    return partners


def gather_kernel(
    q_ref, pk_ref, pv_ref, sk_ref, sv_ref, lay_ref, kv_ref, qall_ref, layall_ref,
    local_sem,
    a_suf_s, a_suf_r, a_pre_s, a_pre_r, a_q_s, a_q_r, a_lay_s, a_lay_r,
    y_suf_s, y_suf_r, y_pre_s, y_pre_r,
    c_suf_s, c_suf_r, c_pre_s, c_pre_r,
):
    at = Place()
    half_rows = BLOCK // 2
    mine = pl.ds(pl.multiple_of(at.core * half_rows, half_rows), half_rows)
    other = pl.ds(pl.multiple_of((1 - at.core) * half_rows, half_rows), half_rows)
    sides = (at.device(dy=1), at.device(dy=3))
    twin = at.device(dc=1)
    meet(plane_partners(at) + [*sides, twin])

    def send(src, dst, send_sem, recv_sem, device):
        pltpu.make_async_remote_copy(
            src_ref=src, dst_ref=dst, send_sem=send_sem, recv_sem=recv_sem, device_id=device, device_id_type=MESH
        ).start()

    def suf_at(dy, member):
        return 32 + lax.rem(at.y + dy, 4) * 8 + member

    def pre_at(dy, member):
        return lax.rem(at.y + dy, 4) * 8 + member

    own_columns = columns(at.member, HEAD_DIM)
    own_k, own_v = sk_ref.at[:, own_columns], sv_ref.at[:, own_columns]
    own_pk, own_pv = pk_ref.at[mine, own_columns], pv_ref.at[mine, own_columns]
    suf_here, pre_here = suf_at(0, at.member), pre_at(0, at.member)

    for t in range(1, UNITS):
        dz, dx = STEPS[t]
        device = at.device(dz=dz, dx=dx)
        there = columns(at.member_at(dz, dx), HEAD_DIM)
        send(sk_ref.at[:, there], kv_ref.at[suf_here, 0], a_suf_s.at[t], a_suf_r.at[t], device)
        send(sv_ref.at[:, there], kv_ref.at[suf_here, 1], a_suf_s.at[t], a_suf_r.at[t], device)
        send(pk_ref.at[mine, there], kv_ref.at[pre_here, 0, mine], a_pre_s.at[t], a_pre_r.at[t], device)
        send(pv_ref.at[mine, there], kv_ref.at[pre_here, 1, mine], a_pre_s.at[t], a_pre_r.at[t], device)
    for way, device in enumerate(sides):
        send(own_k, kv_ref.at[suf_here, 0], y_suf_s.at[way, 0], y_suf_r.at[way, 0], device)
        send(own_v, kv_ref.at[suf_here, 1], y_suf_s.at[way, 0], y_suf_r.at[way, 0], device)
        send(own_pk, kv_ref.at[pre_here, 0, mine], y_pre_s.at[way, 0], y_pre_r.at[way, 0], device)
        send(own_pv, kv_ref.at[pre_here, 1, mine], y_pre_s.at[way, 0], y_pre_r.at[way, 0], device)
    send(own_k, kv_ref.at[suf_here + 32, 0], c_suf_s.at[0, 0], c_suf_r.at[0, 0], twin)
    send(own_v, kv_ref.at[suf_here + 32, 1], c_suf_s.at[0, 0], c_suf_r.at[0, 0], twin)
    send(own_pk, kv_ref.at[pre_here, 0, mine], c_pre_s.at[0, 0], c_pre_r.at[0, 0], twin)
    send(own_pv, kv_ref.at[pre_here, 1, mine], c_pre_s.at[0, 0], c_pre_r.at[0, 0], twin)
    for t in range(1, UNITS):
        dz, dx = STEPS[t]
        device = at.device(dz=dz, dx=dx, dc=dx)
        there = columns(at.member_at(dz, dx), WIDE)
        send(lay_ref, layall_ref.at[at.z * 2 + dx], a_lay_s.at[t], a_lay_r.at[t], device)
        send(q_ref.at[:, there], qall_ref.at[at.z * 2 + dx], a_q_s.at[t], a_q_r.at[t], device)

    q_columns = columns(at.member, WIDE)
    staying = [
        pltpu.make_async_copy(own_k, kv_ref.at[suf_here, 0], local_sem.at[0]),
        pltpu.make_async_copy(own_v, kv_ref.at[suf_here, 1], local_sem.at[1]),
        pltpu.make_async_copy(own_pk, kv_ref.at[pre_here, 0, mine], local_sem.at[2]),
        pltpu.make_async_copy(own_pv, kv_ref.at[pre_here, 1, mine], local_sem.at[3]),
        pltpu.make_async_copy(q_ref.at[:, q_columns], qall_ref.at[at.z * 2], local_sem.at[4]),
        pltpu.make_async_copy(lay_ref, layall_ref.at[at.z * 2], local_sem.at[5]),
    ]
    for copy in staying:
        copy.start()

    def suf_block(dy, member):
        return kv_ref.at[suf_at(dy, member)]

    def pre_block(dy, member, rows=mine):
        return kv_ref.at[pre_at(dy, member), :, rows]

    def arrived(block, sem):
        pltpu.make_async_copy(block, block, sem).wait()

    def source(t):
        dz, dx = STEPS[t]
        return at.member_at(4 - dz, dx)

    def to_twin(dy, t):
        member = source(t)
        place = suf_at(dy, member)
        send(kv_ref.at[place], kv_ref.at[place + 32], c_suf_s.at[dy, t], c_suf_r.at[dy, t], twin)
        block = pre_block(dy, member)
        send(block, block, c_pre_s.at[dy, t], c_pre_r.at[dy, t], twin)

    def from_plane(t):
        if t:
            arrived(suf_block(0, source(t)), a_suf_r.at[t])
            arrived(pre_block(0, source(t)), a_pre_r.at[t])

    def along_y(way, t):
        if t:
            suf, pre = suf_block(0, source(t)), pre_block(0, source(t))
            send(suf, suf, y_suf_s.at[way, t], y_suf_r.at[way, t], sides[way])
            send(pre, pre, y_pre_s.at[way, t], y_pre_r.at[way, t], sides[way])

    def from_side(way, t, relays):
        dy = 3 - 2 * way
        suf, pre = suf_block(dy, source(t)), pre_block(dy, source(t))
        arrived(suf, y_suf_r.at[way, t])
        if relays:
            send(suf, suf, y_suf_s.at[2, t], y_suf_r.at[2, t], sides[way])
        arrived(pre, y_pre_r.at[way, t])
        if relays:
            send(pre, pre, y_pre_s.at[2, t], y_pre_r.at[2, t], sides[way])
        to_twin(dy, t)

    def from_far(t):
        arrived(suf_block(2, source(t)), y_suf_r.at[2, t])
        arrived(pre_block(2, source(t)), y_pre_r.at[2, t])
        to_twin(2, t)

    firsts = ((0, 1, 3, 5), (2, 4, 6, 7))
    for i in range(4):
        for way in range(2):
            from_plane(firsts[way][i])
            along_y(way, firsts[way][i])
    for i in range(4):
        for way in range(2):
            along_y(way, firsts[1 - way][i])
    for i in range(4):
        for way in range(2):
            from_side(way, firsts[way][i], True)
    for t in range(1, UNITS):
        to_twin(0, t)
    for i in range(4):
        for way in range(2):
            from_side(way, firsts[1 - way][i], False)
    for i in range(4):
        for way in range(2):
            from_far(firsts[way][i])

    for t in range(UNITS):
        member = source(t)
        for dy in range(4):
            arrived(kv_ref.at[suf_at(dy, member) + 32], c_suf_r.at[dy, t])
            arrived(pre_block(dy, member, other), c_pre_r.at[dy, t])
    for t in range(1, UNITS):
        dz, dx = STEPS[t]
        slot = lax.rem(at.z + 4 - dz, 4) * 2 + dx
        arrived(qall_ref.at[slot], a_q_r.at[t])
        arrived(layall_ref.at[slot], a_lay_r.at[t])
    suf, pre = suf_block(0, at.member), pre_block(0, at.member)
    for t in range(UNITS):
        if t:
            arrived(suf, a_suf_s.at[t])
            arrived(pre, a_pre_s.at[t])
            arrived(qall_ref.at[at.z * 2], a_q_s.at[t])
            arrived(layall_ref.at[at.z * 2], a_lay_s.at[t])
        for way in range(3):
            arrived(suf, y_suf_s.at[way, t])
            arrived(pre, y_pre_s.at[way, t])
        for dy in range(4):
            arrived(suf, c_suf_s.at[dy, t])
            arrived(pre, c_pre_s.at[dy, t])
    for copy in staying:
        copy.wait()


def gather(queries, prefix_keys, prefix_values, suffix_keys, suffix_values, layout):
    dma = pltpu.SemaphoreType.DMA
    anywhere = pl.BlockSpec(memory_space=pl.ANY)
    return pl.pallas_call(
        gather_kernel,
        name="gather",
        out_shape=(
            pltpu.VMEM((96, 2, BLOCK, HEAD_DIM), BF16),
            pltpu.VMEM((UNITS, BLOCK, WIDE), BF16),
            pltpu.VMEM((UNITS, 1, 128), jnp.int32),
        ),
        in_specs=[pl.BlockSpec(memory_space=pltpu.HBM)] * 6,
        out_specs=(pl.BlockSpec(memory_space=pltpu.VMEM),) * 3,
        scratch_shapes=[
            dma((6,)),
        ]
        + [dma((UNITS,))] * 8
        + [dma((3, UNITS))] * 4
        + [dma((4, UNITS))] * 4,
        compiler_params=pltpu.CompilerParams(vmem_limit_bytes=52 * 2**20, collective_id=0, has_side_effects=True),
    )(queries, prefix_keys, prefix_values, suffix_keys, suffix_values, layout)


def attend_kernel(lay_ref, q_ref, kv_ref, o_ref, table, m_ref, l_ref, acc_ref):
    unit = pl.program_id(0)
    at = Place()
    flip = lax.rem(unit, 2)
    block = ((unit // 2) * 4 + at.y) * 2 + lax.rem(at.x + flip, 2)
    live = block < lay_ref[unit, 64]
    factor = math.log2(math.e) / math.sqrt(HEAD_DIM)

    def place_of(j):
        return ((j // 2) % 4) * 8 + (j // 8) * 2 + j % 2

    @pl.when(jnp.logical_not(live))
    def _():
        o_ref[unit] = jnp.zeros((BLOCK, WIDE), BF16)

    @pl.when(live)
    def _():
        count = jnp.int32(0)
        for j in range(32):
            table[count] = jnp.int32(place_of(j))
            count = count + jnp.where(lay_ref[unit, j] > 0, 1, 0)
        suffix_base = 32 + 32 * flip
        for j in range(32):
            table[count] = suffix_base + place_of(j)
            count = count + jnp.where((lay_ref[unit, 32 + j] > 0) & (j < block), 1, 0)
        diagonal = suffix_base + lax.rem(block // 2, 4) * 8 + (block // 8) * 2 + lax.rem(block, 2)
        spare = lax.rem(count, CHUNK)
        q = jnp.concatenate([q_ref[unit, :, g * HEAD_DIM:(g + 1) * HEAD_DIM] for g in range(GROUP)], axis=0)

        def scores_of(places):
            k = jnp.concatenate([kv_ref[p, 0] for p in places], axis=0)
            return lax.dot_general(q, k, (((1,), (1,)), ((), ())), preferred_element_type=jnp.float32)

        def product(weights, places):
            v = jnp.concatenate([kv_ref[p, 1] for p in places], axis=0)
            return lax.dot_general(
                weights.astype(BF16), v, (((1,), (0,)), ((), ())), preferred_element_type=jnp.float32
            )

        def spread(column, width):
            return jnp.broadcast_to(column, (column.shape[0], width))

        wide = CHUNK * BLOCK
        places = [diagonal]
        for s in range(CHUNK - 1):
            places.append(jnp.where(s < spare, table[s], diagonal))
        s = scores_of(places)
        row = lax.broadcasted_iota(jnp.int32, s.shape, 0) % BLOCK
        col = lax.broadcasted_iota(jnp.int32, s.shape, 1)
        last = jnp.where(col < BLOCK, row, (spare + 1) * BLOCK - 1)
        s = jnp.where(col <= last, s, MASKED)
        top = jnp.max(s, axis=1, keepdims=True)
        weights = jnp.exp2((s - top) * factor)
        m_ref[...] = spread(top, 128)
        l_ref[...] = spread(jnp.sum(weights, axis=1, keepdims=True), 128)
        acc_ref[...] = product(weights, places)

        @pl.loop(0, count // CHUNK)
        def _(step):
            first = spare + step * CHUNK
            places = [table[first + s] for s in range(CHUNK)]
            s = scores_of(places)
            old = m_ref[...]
            new = jnp.maximum(old, spread(jnp.max(s, axis=1, keepdims=True), 128))
            scale = jnp.exp2((old - new) * factor)
            weights = jnp.exp2((s - jnp.concatenate([new] * CHUNK, axis=1)) * factor)
            m_ref[...] = new
            l_ref[...] = l_ref[...] * scale + spread(jnp.sum(weights, axis=1, keepdims=True), 128)
            acc_ref[...] = acc_ref[...] * scale + product(weights, places)

        out = (acc_ref[...] / l_ref[...]).astype(BF16)
        for g in range(GROUP):
            o_ref[unit, :, g * HEAD_DIM:(g + 1) * HEAD_DIM] = out[g * BLOCK:(g + 1) * BLOCK]


def attend(layout, queries, kv):
    rows = GROUP * BLOCK
    return pl.pallas_call(
        attend_kernel,
        name="attend",
        grid=(UNITS,),
        out_shape=pltpu.VMEM((UNITS, BLOCK, WIDE), BF16),
        in_specs=[
            pl.BlockSpec(memory_space=pltpu.SMEM),
            pl.BlockSpec(memory_space=pltpu.VMEM),
            pl.BlockSpec(memory_space=pltpu.VMEM),
        ],
        out_specs=pl.BlockSpec(memory_space=pltpu.VMEM),
        scratch_shapes=[
            pltpu.SMEM((72,), jnp.int32),
            pltpu.VMEM((rows, 128), jnp.float32),
            pltpu.VMEM((rows, 128), jnp.float32),
            pltpu.VMEM((rows, HEAD_DIM), jnp.float32),
        ],
        compiler_params=pltpu.CompilerParams(vmem_limit_bytes=32 * 2**20, dimension_semantics=("arbitrary",)),
    )(layout, queries, kv)


def spread_kernel(part_ref, out_ref, local_sem, send_sem, recv_sem):
    at = Place()
    partners = [at.device(dz=dz, dx=dx, dc=dx) for dz, dx in STEPS[1:]]
    meet(partners)
    here = columns(at.member, WIDE)
    for t in range(1, UNITS):
        dz, dx = STEPS[t]
        pltpu.make_async_remote_copy(
            src_ref=part_ref.at[lax.rem(at.z + dz, 4) * 2 + dx],
            dst_ref=out_ref.at[:, here],
            send_sem=send_sem.at[t],
            recv_sem=recv_sem.at[t],
            device_id=partners[t - 1],
            device_id_type=MESH,
        ).start()
    staying = pltpu.make_async_copy(part_ref.at[at.z * 2], out_ref.at[:, here], local_sem)
    staying.start()
    for t in range(1, UNITS):
        dz, dx = STEPS[t]
        there = out_ref.at[:, columns(at.member_at(4 - dz, dx), WIDE)]
        pltpu.make_async_copy(there, there, recv_sem.at[t]).wait()
        gone = part_ref.at[lax.rem(at.z + dz, 4) * 2 + dx]
        pltpu.make_async_copy(gone, gone, send_sem.at[t]).wait()
    staying.wait()


def spread(parts):
    dma = pltpu.SemaphoreType.DMA
    anywhere = pl.BlockSpec(memory_space=pl.ANY)
    return pl.pallas_call(
        spread_kernel,
        name="spread",
        out_shape=pltpu.VMEM((BLOCK, HEADS * HEAD_DIM), BF16),
        in_specs=[pl.BlockSpec(memory_space=pltpu.VMEM)],
        out_specs=pl.BlockSpec(memory_space=pltpu.VMEM),
        scratch_shapes=[dma, dma((UNITS,)), dma((UNITS,))],
        compiler_params=pltpu.CompilerParams(vmem_limit_bytes=32 * 2**20, collective_id=1, has_side_effects=True),
    )(parts)


def shards(
    queries, prefix_keys, prefix_values, suffix_keys, suffix_values, layout_pre, layout_suf, lengths
):
    layout = jnp.concatenate(
        [layout_pre[0], layout_suf[0], jnp.broadcast_to(lengths[:, None], (1, 64))], axis=1
    )
    kv, q_all, layouts = gather(
        queries[0], prefix_keys, prefix_values, suffix_keys[0], suffix_values[0], layout
    )
    parts = attend(layouts[:, 0], q_all, kv)
    return spread(parts)[None]


def solution(mesh):
    return jax.shard_map(
        shards,
        mesh=mesh,
        in_specs=(
            P("samp", "seq", None),
            P("seq", None),
            P("seq", None),
            P("samp", "seq", None),
            P("samp", "seq", None),
            P("samp", "seq", None),
            P("samp", "seq", None),
            P("samp"),
        ),
        out_specs=P("samp", "seq", None),
        check_vma=False,
    )
```

```python
import math

import jax
import jax.numpy as jnp
from jax import lax
from jax.experimental import pallas as pl
from jax.experimental.pallas import tpu as pltpu
from jax.sharding import PartitionSpec as P

HEADS = 40
KV_HEADS = 8
HEAD_DIM = 128
BLOCK = 128
GROUP = HEADS // KV_HEADS
WIDE = GROUP * HEAD_DIM
CHUNK = 4
EARLY = 1
BEFORE = 3
FIRST = CHUNK * EARLY
UNITS = 8
MASKED = -1e30
MESH = pl.DeviceIdType.MESH
BF16 = jnp.bfloat16

STEPS = tuple((t // 2, t % 2) for t in range(UNITS))


class Place:
    def __init__(self):
        seq = lax.axis_index("seq")
        samp = lax.axis_index("samp")
        self.z = seq // 8
        self.y = lax.rem(seq // 2, 4)
        self.x = lax.rem(seq, 2)
        self.half = samp // 2
        self.core = lax.rem(samp, 2)
        self.member = self.z * 2 + self.x

    def device(self, dz=0, dy=0, dx=0, dc=0):
        z = lax.rem(self.z + dz, 4)
        y = lax.rem(self.y + dy, 4)
        x = lax.rem(self.x + dx, 2)
        core = lax.rem(self.core + dc, 2)
        return ((z * 4 + y) * 2 + x, self.half * 2 + core)

    def member_at(self, dz, dx):
        return lax.rem(self.z + dz, 4) * 2 + lax.rem(self.x + dx, 2)


def columns(member, width):
    return pl.ds(pl.multiple_of(member * width, width), width)


def meet(partners):
    barrier = pltpu.get_barrier_semaphore()
    for partner in partners:
        pl.semaphore_signal(barrier, inc=1, device_id=partner, device_id_type=MESH)
    pl.semaphore_wait(barrier, len(partners))


def plane_partners(at):
    partners = []
    for dz, dx in STEPS[1:]:
        partners.append(at.device(dz=dz, dx=dx))
        if dx:
            partners.append(at.device(dz=dz, dx=dx, dc=1))
    return partners


def place_of(j):
    return ((j // 2) % 4) * 8 + (j // 8) * 2 + j % 2


def plan_kernel(pre_ref, suf_ref, lengths_ref, plan_ref):
    at = Place()
    block = (at.z * 4 + at.y) * 2 + at.x
    for j in range(FIRST):
        plan_ref[0, j] = 0
    end = jnp.int32(0)
    for j in range(32):
        plan_ref[0, end] = place_of(j)
        end = end + jnp.where(pre_ref[0, j] > 0, 1, 0)
    plan_ref[0, 120] = end
    end = jnp.maximum(end, FIRST)
    for j in range(32):
        plan_ref[0, end] = 32 + place_of(j)
        end = end + jnp.where((suf_ref[0, j] > 0) & (j < block), 1, 0)
    plan_ref[0, 121] = end - FIRST
    plan_ref[0, 122] = jnp.where(block < lengths_ref[0], 1, 0)


def plan(layout_pre, layout_suf, lengths):
    smem = pl.BlockSpec(memory_space=pltpu.SMEM)
    return pl.pallas_call(
        plan_kernel,
        name="plan",
        out_shape=jax.ShapeDtypeStruct((1, 128), jnp.int32),
        in_specs=[smem] * 3,
        out_specs=smem,
    )(layout_pre, layout_suf, lengths)


FACTOR = math.log2(math.e) / math.sqrt(HEAD_DIM)


def stacked(q_ref, slot):
    return jnp.concatenate([q_ref[slot, :, g * HEAD_DIM:(g + 1) * HEAD_DIM] for g in range(GROUP)], axis=0)


def spread_over(column):
    return jnp.broadcast_to(column, (column.shape[0], 128))


def scores_of(q, key_blocks):
    k = jnp.concatenate(key_blocks, axis=0)
    return lax.dot_general(q, k, (((1,), (1,)), ((), ())), preferred_element_type=jnp.float32)


def take_in(s, value_blocks, before, after):
    (m_old, l_old, acc_old), (m_ref, l_ref, acc_ref) = before, after
    old = m_old[...]
    new = jnp.maximum(old, spread_over(jnp.max(s, axis=1, keepdims=True)))
    scale = jnp.exp2((old - new) * FACTOR)
    weights = jnp.exp2((s - jnp.concatenate([new] * CHUNK, axis=1)) * FACTOR)
    m_ref[...] = new
    l_ref[...] = l_old[...] * scale + spread_over(jnp.sum(weights, axis=1, keepdims=True))
    acc_ref[...] = acc_old[...] * scale + lax.dot_general(
        weights.astype(BF16), jnp.concatenate(value_blocks, axis=0), (((1,), (0,)), ((), ())),
        preferred_element_type=jnp.float32,
    )


def gather_kernel(
    q_ref, pk_ref, pv_ref, sk_ref, sv_ref, lay_ref, kvs_ref, qall_ref, layall_ref, m_ref, l_ref, acc_ref,
    kvp_ref, plans, local_sem,
    a_suf_s, a_suf_r, a_pre_s, a_pre_r, a_q_s, a_q_r, a_lay_s, a_lay_r,
    y_suf_s, y_suf_r, y_pre_s, y_pre_r,
    c_suf_s, c_suf_r, c_pre_s, c_pre_r,
):
    at = Place()
    half_rows = BLOCK // 2
    mine = pl.ds(pl.multiple_of(at.core * half_rows, half_rows), half_rows)
    other = pl.ds(pl.multiple_of((1 - at.core) * half_rows, half_rows), half_rows)
    sides = (at.device(dy=1), at.device(dy=3))
    twin = at.device(dc=1)
    meet(plane_partners(at) + [*sides, twin])

    def send(src, dst, send_sem, recv_sem, device):
        pltpu.make_async_remote_copy(
            src_ref=src, dst_ref=dst, send_sem=send_sem, recv_sem=recv_sem, device_id=device, device_id_type=MESH
        ).start()

    def suf_at(dy, member):
        return 32 + lax.rem(at.y + dy, 4) * 8 + member

    def pre_at(dy, member):
        return lax.rem(at.y + dy, 4) * 8 + member

    own_columns = columns(at.member, HEAD_DIM)
    own_k, own_v = sk_ref.at[:, own_columns], sv_ref.at[:, own_columns]
    own_pk, own_pv = pk_ref.at[mine, own_columns], pv_ref.at[mine, own_columns]
    suf_here, pre_here = suf_at(0, at.member), pre_at(0, at.member)

    def own_blocks(k, v, ref, places, sems, recvs, device, rows=None):
        for which, part in ((0, k), (1, v)):
            dst = ref.at[places, which] if rows is None else ref.at[places, which, rows]
            send(part, dst, sems, recvs, device)

    for t in range(1, UNITS):
        dz, dx = STEPS[t]
        there = columns(at.member_at(dz, dx), HEAD_DIM)
        own_blocks(pk_ref.at[mine, there], pv_ref.at[mine, there], kvp_ref, pre_here, a_pre_s.at[t], a_pre_r.at[t],
                   at.device(dz=dz, dx=dx), mine)
    for way, device in enumerate(sides):
        own_blocks(own_pk, own_pv, kvp_ref, pre_here, y_pre_s.at[way, 0], y_pre_r.at[way, 0], device, mine)
    own_blocks(own_pk, own_pv, kvp_ref, pre_here, c_pre_s.at[0, 0], c_pre_r.at[0, 0], twin, mine)
    for t in range(1, UNITS):
        dz, dx = STEPS[t]
        there = columns(at.member_at(dz, dx), HEAD_DIM)
        own_blocks(sk_ref.at[:, there], sv_ref.at[:, there], kvs_ref, suf_here, a_suf_s.at[t], a_suf_r.at[t],
                   at.device(dz=dz, dx=dx))
    for t in range(1, UNITS):
        dz, dx = STEPS[t]
        device = at.device(dz=dz, dx=dx, dc=dx)
        there = columns(at.member_at(dz, dx), WIDE)
        send(lay_ref, layall_ref.at[at.z * 2 + dx], a_lay_s.at[t], a_lay_r.at[t], device)
        send(q_ref.at[:, there], qall_ref.at[at.z * 2 + dx], a_q_s.at[t], a_q_r.at[t], device)

    q_columns = columns(at.member, WIDE)
    staying = [
        pltpu.make_async_copy(own_k, kvs_ref.at[suf_here, 0], local_sem.at[0]),
        pltpu.make_async_copy(own_v, kvs_ref.at[suf_here, 1], local_sem.at[1]),
        pltpu.make_async_copy(own_pk, kvp_ref.at[pre_here, 0, mine], local_sem.at[2]),
        pltpu.make_async_copy(own_pv, kvp_ref.at[pre_here, 1, mine], local_sem.at[3]),
        pltpu.make_async_copy(q_ref.at[:, q_columns], qall_ref.at[at.z * 2], local_sem.at[4]),
        pltpu.make_async_copy(lay_ref, layall_ref.at[at.z * 2], local_sem.at[5]),
    ]
    for copy in staying:
        copy.start()

    def arrived(block, sem):
        pltpu.make_async_copy(block, block, sem).wait()

    def source(t):
        return at.member_at(4 - t // 2, t % 2)

    def suf_block(dy, t):
        return kvs_ref.at[suf_at(dy, source(t))]

    def pre_block(dy, t, rows=mine):
        return kvp_ref.at[pre_at(dy, source(t)), :, rows]

    def suf_to_twin(dy, t):
        place = suf_at(dy, source(t))
        send(kvs_ref.at[place], kvs_ref.at[place + 32], c_suf_s.at[dy, t], c_suf_r.at[dy, t], twin)

    def pre_to_twin(dy, t):
        block = pre_block(dy, t)
        send(block, block, c_pre_s.at[dy, t], c_pre_r.at[dy, t], twin)

    def side(way):
        return at.device(dy=1 + 2 * way)

    def pre_from_side(way, t, relays):
        block = pre_block(3 - 2 * way, t)
        arrived(block, y_pre_r.at[way, t])
        if relays:
            send(block, block, y_pre_s.at[2, t], y_pre_r.at[2, t], side(way))
        pre_to_twin(3 - 2 * way, t)

    def suf_from_side(way, t, relays):
        block = suf_block(3 - 2 * way, t)
        arrived(block, y_suf_r.at[way, t])
        if relays:
            send(block, block, y_suf_s.at[2, t], y_suf_r.at[2, t], side(way))
        suf_to_twin(3 - 2 * way, t)

    def both(count=4):
        return [(way, 4 * way + i) for i in range(count) for way in range(2)]

    def along(way, t, block, send_sem, recv_sem):
        if t:
            send(block, block, send_sem.at[way, t], recv_sem.at[way, t], sides[way])

    for way, t in both():
        if t:
            arrived(pre_block(0, t), a_pre_r.at[t])
        along(way, t, pre_block(0, t), y_pre_s, y_pre_r)
    for way, t in both():
        along(1 - way, t, pre_block(0, t), y_pre_s, y_pre_r)
    for way, t in both():
        pre_from_side(way, t, True)
    own_blocks(own_k, own_v, kvs_ref, suf_here, y_suf_s.at[0, 0], y_suf_r.at[0, 0], sides[0])
    for way, t in both():
        if t:
            arrived(suf_block(0, t), a_suf_r.at[t])
        along(way, t, suf_block(0, t), y_suf_s, y_suf_r)
    own_blocks(own_k, own_v, kvs_ref, suf_here, y_suf_s.at[1, 0], y_suf_r.at[1, 0], sides[1])
    for way, t in both():
        along(1 - way, t, suf_block(0, t), y_suf_s, y_suf_r)
    for t in range(1, UNITS):
        pre_to_twin(0, t)
    own_blocks(own_k, own_v, kvs_ref, suf_here + 32, c_suf_s.at[0, 0], c_suf_r.at[0, 0], twin)
    for t in range(1, UNITS):
        suf_to_twin(0, t)
    for way, t in both():
        pre_from_side(1 - way, t, False)
    for t in range(UNITS):
        arrived(pre_block(2, t), y_pre_r.at[2, t])
        pre_to_twin(2, t)
    for t in range(UNITS):
        for dy in range(4):
            arrived(pre_block(dy, t, other), c_pre_r.at[dy, t])

    def slot_of(t):
        return lax.rem(at.z + 4 - t // 2, 4) * 2 + t % 2

    for t in range(1, UNITS):
        arrived(layall_ref.at[slot_of(t)], a_lay_r.at[t])
    for copy in staying:
        copy.wait()
    copy = pltpu.make_async_copy(layall_ref, plans, local_sem.at[6])
    copy.start()
    copy.wait()

    keep = pltpu.make_async_copy(kvp_ref, kvs_ref.at[pl.ds(0, 32)], local_sem.at[7])
    keep.start()

    def first_blocks(t):
        slot = slot_of(t)
        q = stacked(qall_ref, slot)
        m, l, acc = m_ref.at[slot], l_ref.at[slot], acc_ref.at[slot]
        m[...] = jnp.full((GROUP * BLOCK, 128), MASKED, jnp.float32)
        l[...] = jnp.zeros((GROUP * BLOCK, 128), jnp.float32)
        acc[...] = jnp.zeros((GROUP * BLOCK, HEAD_DIM), jnp.float32)
        valid = plans[slot, 0, 120]

        @pl.loop(0, EARLY)
        def _(step):
            places = [plans[slot, 0, step * CHUNK + i] for i in range(CHUNK)]
            s = scores_of(q, [kvp_ref[p, 0] for p in places])
            col = lax.broadcasted_iota(jnp.int32, (1, CHUNK * BLOCK), 1)
            s = s + jnp.where(col < (valid - step * CHUNK) * BLOCK, 0.0, MASKED)
            take_in(s, [kvp_ref[p, 1] for p in places], (m, l, acc), (m, l, acc))

    @pl.loop(0, BEFORE)
    def _(t):
        @pl.when(t > 0)
        def _():
            arrived(qall_ref.at[slot_of(t)], a_q_r.at[t])
        first_blocks(t)

    for way, t in both():
        suf_from_side(way, t, True)

    @pl.loop(BEFORE, UNITS)
    def _(t):
        arrived(qall_ref.at[slot_of(t)], a_q_r.at[t])
        first_blocks(t)

    for way, t in both():
        suf_from_side(1 - way, t, False)
    for t in range(UNITS):
        arrived(suf_block(2, t), y_suf_r.at[2, t])
        suf_to_twin(2, t)

    keep.wait()
    for t in range(UNITS):
        for dy in range(4):
            arrived(kvs_ref.at[suf_at(dy, source(t)) + 32], c_suf_r.at[dy, t])
    suf, pre = suf_block(0, 0), pre_block(0, 0)
    for t in range(UNITS):
        if t:
            arrived(suf, a_suf_s.at[t])
            arrived(pre, a_pre_s.at[t])
            arrived(qall_ref.at[at.z * 2], a_q_s.at[t])
            arrived(layall_ref.at[at.z * 2], a_lay_s.at[t])
        for way in range(3):
            arrived(suf, y_suf_s.at[way, t])
            arrived(pre, y_pre_s.at[way, t])
        for dy in range(4):
            arrived(suf, c_suf_s.at[dy, t])
            arrived(pre, c_pre_s.at[dy, t])


def gather(queries, prefix_keys, prefix_values, suffix_keys, suffix_values, layout):
    dma = pltpu.SemaphoreType.DMA
    anywhere = pl.BlockSpec(memory_space=pl.ANY)
    return pl.pallas_call(
        gather_kernel,
        name="gather",
        out_shape=(
            pltpu.VMEM((96, 2, BLOCK, HEAD_DIM), BF16),
            pltpu.VMEM((UNITS, BLOCK, WIDE), BF16),
            pltpu.VMEM((UNITS, 1, 128), jnp.int32),
            pltpu.VMEM((UNITS, GROUP * BLOCK, 128), jnp.float32),
            pltpu.VMEM((UNITS, GROUP * BLOCK, 128), jnp.float32),
            pltpu.VMEM((UNITS, GROUP * BLOCK, HEAD_DIM), jnp.float32),
        ),
        in_specs=[pl.BlockSpec(memory_space=pltpu.HBM)] * 6,
        out_specs=(pl.BlockSpec(memory_space=pltpu.VMEM),) * 6,
        scratch_shapes=[
            pltpu.VMEM((32, 2, BLOCK, HEAD_DIM), BF16),
            pltpu.SMEM((UNITS, 1, 128), jnp.int32),
            dma((8,)),
        ]
        + [dma((UNITS,))] * 8
        + [dma((3, UNITS))] * 4
        + [dma((4, UNITS))] * 4,
        compiler_params=pltpu.CompilerParams(vmem_limit_bytes=40 * 2**20, collective_id=0, has_side_effects=True),
    )(queries, prefix_keys, prefix_values, suffix_keys, suffix_values, layout)


def attend_kernel(plan_ref, q_ref, kv_ref, m_ref, l_ref, acc_ref, o_ref, *sums):
    unit = pl.program_id(0)
    at = Place()
    flip = lax.rem(unit, 2)
    block = ((unit // 2) * 4 + at.y) * 2 + lax.rem(at.x + flip, 2)
    live = plan_ref[unit, 122] > 0

    @pl.when(jnp.logical_not(live))
    def _():
        o_ref[unit] = jnp.zeros((BLOCK, WIDE), BF16)

    @pl.when(live)
    def _():
        count = plan_ref[unit, 121]
        shift = 32 * flip
        diagonal = 32 + shift + lax.rem(block // 2, 4) * 8 + (block // 8) * 2 + lax.rem(block, 2)
        spare = lax.rem(count, CHUNK)
        q = stacked(q_ref, unit)
        begun = m_ref.at[unit], l_ref.at[unit], acc_ref.at[unit]

        def entry(at_entry):
            place = plan_ref[unit, FIRST + at_entry]
            return jnp.where(place < 32, place, place + shift)

        places = [diagonal] + [jnp.where(s < spare, entry(s), diagonal) for s in range(CHUNK - 1)]
        s = scores_of(q, [kv_ref[p, 0] for p in places])
        row = lax.broadcasted_iota(jnp.int32, s.shape, 0) % BLOCK
        col = lax.broadcasted_iota(jnp.int32, s.shape, 1)
        last = jnp.where(col < BLOCK, row, (spare + 1) * BLOCK - 1)
        take_in(jnp.where(col <= last, s, MASKED), [kv_ref[p, 1] for p in places], begun, sums)

        @pl.loop(0, count // CHUNK)
        def _(step):
            places = [entry(spare + step * CHUNK + s) for s in range(CHUNK)]
            s = scores_of(q, [kv_ref[p, 0] for p in places])
            take_in(s, [kv_ref[p, 1] for p in places], sums, sums)

        out = (sums[2][...] / sums[1][...]).astype(BF16)
        for g in range(GROUP):
            o_ref[unit, :, g * HEAD_DIM:(g + 1) * HEAD_DIM] = out[g * BLOCK:(g + 1) * BLOCK]


def attend(plans, queries, kv, begun):
    rows = GROUP * BLOCK
    vmem = pl.BlockSpec(memory_space=pltpu.VMEM)
    return pl.pallas_call(
        attend_kernel,
        name="attend",
        grid=(UNITS,),
        out_shape=pltpu.VMEM((UNITS, BLOCK, WIDE), BF16),
        in_specs=[pl.BlockSpec(memory_space=pltpu.SMEM)] + [vmem] * 5,
        out_specs=vmem,
        scratch_shapes=[pltpu.VMEM((rows, 128), jnp.float32)] * 3,
        compiler_params=pltpu.CompilerParams(
            vmem_limit_bytes=24 * 2**20, dimension_semantics=("arbitrary",)
        ),
    )(plans, queries, kv, *begun)


def spread_kernel(part_ref, out_ref, local_sem, send_sem, recv_sem):
    at = Place()
    partners = [at.device(dz=dz, dx=dx, dc=dx) for dz, dx in STEPS[1:]]
    meet(partners)
    here = columns(at.member, WIDE)
    for t in range(1, UNITS):
        dz, dx = STEPS[t]
        pltpu.make_async_remote_copy(
            src_ref=part_ref.at[lax.rem(at.z + dz, 4) * 2 + dx],
            dst_ref=out_ref.at[:, here],
            send_sem=send_sem.at[t],
            recv_sem=recv_sem.at[t],
            device_id=partners[t - 1],
            device_id_type=MESH,
        ).start()
    staying = pltpu.make_async_copy(part_ref.at[at.z * 2], out_ref.at[:, here], local_sem)
    staying.start()
    for t in range(1, UNITS):
        dz, dx = STEPS[t]
        there = out_ref.at[:, columns(at.member_at(4 - dz, dx), WIDE)]
        pltpu.make_async_copy(there, there, recv_sem.at[t]).wait()
        gone = part_ref.at[lax.rem(at.z + dz, 4) * 2 + dx]
        pltpu.make_async_copy(gone, gone, send_sem.at[t]).wait()
    staying.wait()


def spread(parts):
    dma = pltpu.SemaphoreType.DMA
    anywhere = pl.BlockSpec(memory_space=pl.ANY)
    return pl.pallas_call(
        spread_kernel,
        name="spread",
        out_shape=pltpu.VMEM((BLOCK, HEADS * HEAD_DIM), BF16),
        in_specs=[pl.BlockSpec(memory_space=pltpu.VMEM)],
        out_specs=pl.BlockSpec(memory_space=pltpu.VMEM),
        scratch_shapes=[dma, dma((UNITS,)), dma((UNITS,))],
        compiler_params=pltpu.CompilerParams(vmem_limit_bytes=32 * 2**20, collective_id=1, has_side_effects=True),
    )(parts)


def shards(
    queries, prefix_keys, prefix_values, suffix_keys, suffix_values, layout_pre, layout_suf, lengths
):
    kv, q_all, plans, *begun = gather(
        queries[0], prefix_keys, prefix_values, suffix_keys[0], suffix_values[0],
        plan(layout_pre[0], layout_suf[0], lengths),
    )
    parts = attend(plans[:, 0], q_all, kv, begun)
    return spread(parts)[None]


def solution(mesh):
    return jax.shard_map(
        shards,
        mesh=mesh,
        in_specs=(
            P("samp", "seq", None),
            P("seq", None),
            P("seq", None),
            P("samp", "seq", None),
            P("samp", "seq", None),
            P("samp", "seq", None),
            P("samp", "seq", None),
            P("samp"),
        ),
        out_specs=P("samp", "seq", None),
        check_vma=False,
    )
```

```python
import math

import jax
import jax.numpy as jnp
from jax import lax
from jax.experimental import pallas as pl
from jax.experimental.pallas import tpu as pltpu
from jax.sharding import PartitionSpec as P

HEADS = 40
KV_HEADS = 8
HEAD_DIM = 128
BLOCK = 128
GROUP = HEADS // KV_HEADS
WIDE = GROUP * HEAD_DIM
CHUNK = 4
EARLY = 1
BEFORE = 3
ATTEND_MIB = 24
LEAVING = (5, 3, 7, 4, 1, 2, 6, 0)
FIRST = CHUNK * EARLY
UNITS = 8
MASKED = -1e30
MESH = pl.DeviceIdType.MESH
BF16 = jnp.bfloat16

STEPS = tuple((t // 2, t % 2) for t in range(UNITS))


class Place:
    def __init__(self):
        seq = lax.axis_index("seq")
        samp = lax.axis_index("samp")
        self.z = seq // 8
        self.y = lax.rem(seq // 2, 4)
        self.x = lax.rem(seq, 2)
        self.half = samp // 2
        self.core = lax.rem(samp, 2)
        self.member = self.z * 2 + self.x

    def device(self, dz=0, dy=0, dx=0, dc=0):
        z = lax.rem(self.z + dz, 4)
        y = lax.rem(self.y + dy, 4)
        x = lax.rem(self.x + dx, 2)
        core = lax.rem(self.core + dc, 2)
        return ((z * 4 + y) * 2 + x, self.half * 2 + core)

    def member_at(self, dz, dx):
        return lax.rem(self.z + dz, 4) * 2 + lax.rem(self.x + dx, 2)


def columns(member, width):
    return pl.ds(pl.multiple_of(member * width, width), width)


def meet(partners):
    barrier = pltpu.get_barrier_semaphore()
    for partner in partners:
        pl.semaphore_signal(barrier, inc=1, device_id=partner, device_id_type=MESH)
    pl.semaphore_wait(barrier, len(partners))


def plane_partners(at):
    partners = []
    for dz, dx in STEPS[1:]:
        partners.append(at.device(dz=dz, dx=dx))
        if dx:
            partners.append(at.device(dz=dz, dx=dx, dc=1))
    return partners


def place_of(j):
    return ((j // 2) % 4) * 8 + (j // 8) * 2 + j % 2


def plan_kernel(pre_ref, suf_ref, lengths_ref, plan_ref):
    at = Place()
    block = (at.z * 4 + at.y) * 2 + at.x
    for j in range(FIRST):
        plan_ref[0, j] = 0
    end = jnp.int32(0)
    for j in range(32):
        plan_ref[0, end] = place_of(j)
        end = end + jnp.where(pre_ref[0, j] > 0, 1, 0)
    plan_ref[0, 120] = end
    end = jnp.maximum(end, FIRST)
    for j in range(32):
        plan_ref[0, end] = 32 + place_of(j)
        end = end + jnp.where((suf_ref[0, j] > 0) & (j < block), 1, 0)
    plan_ref[0, 121] = end - FIRST
    plan_ref[0, 122] = jnp.where(block < lengths_ref[0], 1, 0)


def plan(layout_pre, layout_suf, lengths):
    smem = pl.BlockSpec(memory_space=pltpu.SMEM)
    return pl.pallas_call(
        plan_kernel,
        name="plan",
        out_shape=jax.ShapeDtypeStruct((1, 128), jnp.int32),
        in_specs=[smem] * 3,
        out_specs=smem,
    )(layout_pre, layout_suf, lengths)


FACTOR = math.log2(math.e) / math.sqrt(HEAD_DIM)


def stacked(q_ref, slot):
    return jnp.concatenate([q_ref[slot, :, g * HEAD_DIM:(g + 1) * HEAD_DIM] for g in range(GROUP)], axis=0)


def spread_over(column):
    return jnp.broadcast_to(column, (column.shape[0], 128))


def scores_of(q, key_blocks):
    k = jnp.concatenate(key_blocks, axis=0)
    return lax.dot_general(q, k, (((1,), (1,)), ((), ())), preferred_element_type=jnp.float32)


def take_in(s, value_blocks, before, after):
    (m_old, l_old, acc_old), (m_ref, l_ref, acc_ref) = before, after
    old = m_old[...]
    new = jnp.maximum(old, spread_over(jnp.max(s, axis=1, keepdims=True)))
    scale = jnp.exp2((old - new) * FACTOR)
    weights = jnp.exp2((s - jnp.concatenate([new] * CHUNK, axis=1)) * FACTOR)
    m_ref[...] = new
    l_ref[...] = l_old[...] * scale + spread_over(jnp.sum(weights, axis=1, keepdims=True))
    acc_ref[...] = acc_old[...] * scale + lax.dot_general(
        weights.astype(BF16), jnp.concatenate(value_blocks, axis=0), (((1,), (0,)), ((), ())),
        preferred_element_type=jnp.float32,
    )


def gather_kernel(
    q_ref, pk_ref, pv_ref, sk_ref, sv_ref, lay_ref, kvs_ref, qall_ref, layall_ref, m_ref, l_ref, acc_ref,
    kvp_ref, plans, local_sem,
    a_suf_s, a_suf_r, a_pre_s, a_pre_r, a_q_s, a_q_r, a_lay_s, a_lay_r,
    y_suf_s, y_suf_r, y_pre_s, y_pre_r,
    c_suf_s, c_suf_r, c_pre_s, c_pre_r,
):
    at = Place()
    half_rows = BLOCK // 2
    mine = pl.ds(pl.multiple_of(at.core * half_rows, half_rows), half_rows)
    other = pl.ds(pl.multiple_of((1 - at.core) * half_rows, half_rows), half_rows)
    sides = (at.device(dy=1), at.device(dy=3))
    twin = at.device(dc=1)
    meet(plane_partners(at) + [*sides, twin])

    def send(src, dst, send_sem, recv_sem, device):
        pltpu.make_async_remote_copy(
            src_ref=src, dst_ref=dst, send_sem=send_sem, recv_sem=recv_sem, device_id=device, device_id_type=MESH
        ).start()

    def suf_at(dy, member):
        return 32 + lax.rem(at.y + dy, 4) * 8 + member

    def pre_at(dy, member):
        return lax.rem(at.y + dy, 4) * 8 + member

    own_columns = columns(at.member, HEAD_DIM)
    own_k, own_v = sk_ref.at[:, own_columns], sv_ref.at[:, own_columns]
    own_pk, own_pv = pk_ref.at[mine, own_columns], pv_ref.at[mine, own_columns]
    suf_here, pre_here = suf_at(0, at.member), pre_at(0, at.member)

    def own_blocks(k, v, ref, places, sems, recvs, device, rows=None):
        for which, part in ((0, k), (1, v)):
            dst = ref.at[places, which] if rows is None else ref.at[places, which, rows]
            send(part, dst, sems, recvs, device)

    for t in range(1, UNITS):
        dz, dx = STEPS[t]
        there = columns(at.member_at(dz, dx), HEAD_DIM)
        own_blocks(pk_ref.at[mine, there], pv_ref.at[mine, there], kvp_ref, pre_here, a_pre_s.at[t], a_pre_r.at[t],
                   at.device(dz=dz, dx=dx), mine)
    for way, device in enumerate(sides):
        own_blocks(own_pk, own_pv, kvp_ref, pre_here, y_pre_s.at[way, 0], y_pre_r.at[way, 0], device, mine)
    own_blocks(own_pk, own_pv, kvp_ref, pre_here, c_pre_s.at[0, 0], c_pre_r.at[0, 0], twin, mine)
    for t in range(1, UNITS):
        dz, dx = STEPS[t]
        there = columns(at.member_at(dz, dx), HEAD_DIM)
        own_blocks(sk_ref.at[:, there], sv_ref.at[:, there], kvs_ref, suf_here, a_suf_s.at[t], a_suf_r.at[t],
                   at.device(dz=dz, dx=dx))
    for t in range(1, UNITS):
        dz, dx = STEPS[t]
        device = at.device(dz=dz, dx=dx, dc=dx)
        there = columns(at.member_at(dz, dx), WIDE)
        send(lay_ref, layall_ref.at[at.z * 2 + dx], a_lay_s.at[t], a_lay_r.at[t], device)
        send(q_ref.at[:, there], qall_ref.at[at.z * 2 + dx], a_q_s.at[t], a_q_r.at[t], device)

    q_columns = columns(at.member, WIDE)
    staying = [
        pltpu.make_async_copy(own_k, kvs_ref.at[suf_here, 0], local_sem.at[0]),
        pltpu.make_async_copy(own_v, kvs_ref.at[suf_here, 1], local_sem.at[1]),
        pltpu.make_async_copy(own_pk, kvp_ref.at[pre_here, 0, mine], local_sem.at[2]),
        pltpu.make_async_copy(own_pv, kvp_ref.at[pre_here, 1, mine], local_sem.at[3]),
        pltpu.make_async_copy(q_ref.at[:, q_columns], qall_ref.at[at.z * 2], local_sem.at[4]),
        pltpu.make_async_copy(lay_ref, layall_ref.at[at.z * 2], local_sem.at[5]),
    ]
    for copy in staying:
        copy.start()

    def arrived(block, sem):
        pltpu.make_async_copy(block, block, sem).wait()

    def source(t):
        return at.member_at(4 - t // 2, t % 2)

    def suf_block(dy, t):
        return kvs_ref.at[suf_at(dy, source(t))]

    def pre_block(dy, t, rows=mine):
        return kvp_ref.at[pre_at(dy, source(t)), :, rows]

    def suf_to_twin(dy, t):
        place = suf_at(dy, source(t))
        send(kvs_ref.at[place], kvs_ref.at[place + 32], c_suf_s.at[dy, t], c_suf_r.at[dy, t], twin)

    def pre_to_twin(dy, t):
        block = pre_block(dy, t)
        send(block, block, c_pre_s.at[dy, t], c_pre_r.at[dy, t], twin)

    def side(way):
        return at.device(dy=1 + 2 * way)

    def pre_from_side(way, t, relays):
        block = pre_block(3 - 2 * way, t)
        arrived(block, y_pre_r.at[way, t])
        if relays:
            send(block, block, y_pre_s.at[2, t], y_pre_r.at[2, t], side(way))
        pre_to_twin(3 - 2 * way, t)

    def suf_from_side(way, t, relays):
        block = suf_block(3 - 2 * way, t)
        arrived(block, y_suf_r.at[way, t])
        if relays:
            send(block, block, y_suf_s.at[2, t], y_suf_r.at[2, t], side(way))
        suf_to_twin(3 - 2 * way, t)

    def both(count=4):
        return [(way, 4 * way + i) for i in range(count) for way in range(2)]

    def along(way, t, block, send_sem, recv_sem):
        if t:
            send(block, block, send_sem.at[way, t], recv_sem.at[way, t], sides[way])

    for way, t in both():
        if t:
            arrived(pre_block(0, t), a_pre_r.at[t])
        along(way, t, pre_block(0, t), y_pre_s, y_pre_r)
    for way, t in both():
        along(1 - way, t, pre_block(0, t), y_pre_s, y_pre_r)
    for way, t in both():
        pre_from_side(way, t, True)
    own_blocks(own_k, own_v, kvs_ref, suf_here, y_suf_s.at[0, 0], y_suf_r.at[0, 0], sides[0])
    for way, t in both():
        if t:
            arrived(suf_block(0, t), a_suf_r.at[t])
        along(way, t, suf_block(0, t), y_suf_s, y_suf_r)
    own_blocks(own_k, own_v, kvs_ref, suf_here, y_suf_s.at[1, 0], y_suf_r.at[1, 0], sides[1])
    for way, t in both():
        along(1 - way, t, suf_block(0, t), y_suf_s, y_suf_r)
    for t in range(1, UNITS):
        pre_to_twin(0, t)
    own_blocks(own_k, own_v, kvs_ref, suf_here + 32, c_suf_s.at[0, 0], c_suf_r.at[0, 0], twin)
    for t in range(1, UNITS):
        suf_to_twin(0, t)
    for way, t in both():
        pre_from_side(1 - way, t, False)
    for t in range(UNITS):
        arrived(pre_block(2, t), y_pre_r.at[2, t])
        pre_to_twin(2, t)
    for t in range(UNITS):
        for dy in range(4):
            arrived(pre_block(dy, t, other), c_pre_r.at[dy, t])

    def slot_of(t):
        return lax.rem(at.z + 4 - t // 2, 4) * 2 + t % 2

    for t in range(1, UNITS):
        arrived(layall_ref.at[slot_of(t)], a_lay_r.at[t])
    for copy in staying:
        copy.wait()
    copy = pltpu.make_async_copy(layall_ref, plans, local_sem.at[6])
    copy.start()
    copy.wait()

    keep = pltpu.make_async_copy(kvp_ref, kvs_ref.at[pl.ds(0, 32)], local_sem.at[7])
    keep.start()

    def first_blocks(t):
        slot = slot_of(t)
        q = stacked(qall_ref, slot)
        m, l, acc = m_ref.at[slot], l_ref.at[slot], acc_ref.at[slot]
        m[...] = jnp.full((GROUP * BLOCK, 128), MASKED, jnp.float32)
        l[...] = jnp.zeros((GROUP * BLOCK, 128), jnp.float32)
        acc[...] = jnp.zeros((GROUP * BLOCK, HEAD_DIM), jnp.float32)
        valid = plans[slot, 0, 120]

        @pl.loop(0, EARLY)
        def _(step):
            places = [plans[slot, 0, step * CHUNK + i] for i in range(CHUNK)]
            s = scores_of(q, [kvp_ref[p, 0] for p in places])
            col = lax.broadcasted_iota(jnp.int32, (1, CHUNK * BLOCK), 1)
            s = s + jnp.where(col < (valid - step * CHUNK) * BLOCK, 0.0, MASKED)
            take_in(s, [kvp_ref[p, 1] for p in places], (m, l, acc), (m, l, acc))

    @pl.loop(0, BEFORE)
    def _(t):
        @pl.when(t > 0)
        def _():
            arrived(qall_ref.at[slot_of(t)], a_q_r.at[t])
        first_blocks(t)

    for way, t in both():
        suf_from_side(way, t, True)

    @pl.loop(BEFORE, UNITS)
    def _(t):
        arrived(qall_ref.at[slot_of(t)], a_q_r.at[t])
        first_blocks(t)

    for way, t in both():
        suf_from_side(1 - way, t, False)
    for t in range(UNITS):
        arrived(suf_block(2, t), y_suf_r.at[2, t])
        suf_to_twin(2, t)

    keep.wait()
    for t in range(UNITS):
        for dy in range(4):
            arrived(kvs_ref.at[suf_at(dy, source(t)) + 32], c_suf_r.at[dy, t])
    suf, pre = suf_block(0, 0), pre_block(0, 0)
    for t in range(UNITS):
        if t:
            arrived(suf, a_suf_s.at[t])
            arrived(pre, a_pre_s.at[t])
            arrived(qall_ref.at[at.z * 2], a_q_s.at[t])
            arrived(layall_ref.at[at.z * 2], a_lay_s.at[t])
        for way in range(3):
            arrived(suf, y_suf_s.at[way, t])
            arrived(pre, y_pre_s.at[way, t])
        for dy in range(4):
            arrived(suf, c_suf_s.at[dy, t])
            arrived(pre, c_pre_s.at[dy, t])


def gather(queries, prefix_keys, prefix_values, suffix_keys, suffix_values, layout):
    dma = pltpu.SemaphoreType.DMA
    anywhere = pl.BlockSpec(memory_space=pl.ANY)
    return pl.pallas_call(
        gather_kernel,
        name="gather",
        out_shape=(
            pltpu.VMEM((96, 2, BLOCK, HEAD_DIM), BF16),
            pltpu.VMEM((UNITS, BLOCK, WIDE), BF16),
            pltpu.VMEM((UNITS, 1, 128), jnp.int32),
            pltpu.VMEM((UNITS, GROUP * BLOCK, 128), jnp.float32),
            pltpu.VMEM((UNITS, GROUP * BLOCK, 128), jnp.float32),
            pltpu.VMEM((UNITS, GROUP * BLOCK, HEAD_DIM), jnp.float32),
        ),
        in_specs=[pl.BlockSpec(memory_space=pltpu.HBM)] * 6,
        out_specs=(pl.BlockSpec(memory_space=pltpu.VMEM),) * 6,
        scratch_shapes=[
            pltpu.VMEM((32, 2, BLOCK, HEAD_DIM), BF16),
            pltpu.SMEM((UNITS, 1, 128), jnp.int32),
            dma((8,)),
        ]
        + [dma((UNITS,))] * 8
        + [dma((3, UNITS))] * 4
        + [dma((4, UNITS))] * 4,
        compiler_params=pltpu.CompilerParams(vmem_limit_bytes=40 * 2**20, collective_id=0, has_side_effects=True),
    )(queries, prefix_keys, prefix_values, suffix_keys, suffix_values, layout)


def entry_of(plan_ref, slot, at_entry):
    place = plan_ref[slot, FIRST + at_entry]
    return jnp.where(place < 32, place, place + 32 * lax.rem(slot, 2))


def attend_kernel(plan_ref, q_ref, kv_ref, m_in, l_in, acc_in, m_out, l_out, acc_out):
    unit = pl.program_id(0)

    @pl.when(plan_ref[unit, 122] > 0)
    def _():
        count = plan_ref[unit, 121]
        spare = lax.rem(count, CHUNK)
        q = stacked(q_ref, unit)
        sums = m_out.at[unit], l_out.at[unit], acc_out.at[unit]
        for before, after in zip((m_in, l_in, acc_in), sums):
            after[...] = before[unit]

        @pl.loop(0, count // CHUNK)
        def _(step):
            places = [entry_of(plan_ref, unit, spare + step * CHUNK + s) for s in range(CHUNK)]
            s = scores_of(q, [kv_ref[p, 0] for p in places])
            take_in(s, [kv_ref[p, 1] for p in places], sums, sums)


def attend(plans, queries, kv, begun):
    vmem = pl.BlockSpec(memory_space=pltpu.VMEM)
    return pl.pallas_call(
        attend_kernel,
        name="attend",
        grid=(UNITS,),
        out_shape=(pltpu.VMEM((UNITS, GROUP * BLOCK, 128), jnp.float32),) * 3,
        in_specs=[pl.BlockSpec(memory_space=pltpu.SMEM)] + [vmem] * 5,
        out_specs=(vmem,) * 3,
        compiler_params=pltpu.CompilerParams(
            vmem_limit_bytes=ATTEND_MIB * 2**20, dimension_semantics=("arbitrary",)
        ),
    )(plans, queries, kv, *begun)


def spread_kernel(
    plan_ref, q_ref, kv_ref, m_ref, l_ref, acc_ref, out_ref, part_ref, m_end, l_end, acc_end, local_sem, send_sem, recv_sem
):
    at = Place()
    barrier = pltpu.get_barrier_semaphore()
    for dz, dx in STEPS[1:]:
        pl.semaphore_signal(barrier, inc=1, device_id=at.device(dz=dz, dx=dx, dc=dx), device_id_type=MESH)
    here = columns(at.member, WIDE)

    def slot_of(t):
        return lax.rem(at.z + t // 2, 4) * 2 + t % 2

    def last_blocks(t):
        slot = slot_of(t)
        z, x = lax.rem(at.z + t // 2, 4), lax.rem(at.x + t % 2, 2)
        diagonal = 32 + 32 * (t % 2) + at.y * 8 + z * 2 + x
        spare = lax.rem(plan_ref[slot, 121], CHUNK)
        places = [diagonal]
        for s in range(CHUNK - 1):
            places.append(jnp.where(s < spare, entry_of(plan_ref, slot, s), diagonal))
        s = scores_of(stacked(q_ref, slot), [kv_ref[p, 0] for p in places])
        row = lax.broadcasted_iota(jnp.int32, s.shape, 0) % BLOCK
        col = lax.broadcasted_iota(jnp.int32, s.shape, 1)
        last = jnp.where(col < BLOCK, row, (spare + 1) * BLOCK - 1)
        take_in(
            jnp.where(col <= last, s, MASKED), [kv_ref[p, 1] for p in places],
            (m_ref.at[slot], l_ref.at[slot], acc_ref.at[slot]), (m_end, l_end, acc_end),
        )
        out = jnp.where(plan_ref[slot, 122] > 0, acc_end[...] / l_end[...], 0.0).astype(BF16)
        for g in range(GROUP):
            part_ref[slot, :, g * HEAD_DIM:(g + 1) * HEAD_DIM] = out[g * BLOCK:(g + 1) * BLOCK]

    for i, t in enumerate(LEAVING):
        last_blocks(t)
        if i == 0:
            pl.semaphore_wait(barrier, UNITS - 1)
            continue
        gone = LEAVING[i - 1]
        pltpu.make_async_remote_copy(
            src_ref=part_ref.at[slot_of(gone)],
            dst_ref=out_ref.at[:, here],
            send_sem=send_sem.at[gone],
            recv_sem=recv_sem.at[gone],
            device_id=at.device(dz=gone // 2, dx=gone % 2, dc=gone % 2),
            device_id_type=MESH,
        ).start()

    def arrived(t):
        there = out_ref.at[:, columns(at.member_at(4 - t // 2, t % 2), WIDE)]
        pltpu.make_async_copy(there, there, recv_sem.at[t]).wait()

    arrived(LEAVING[0])
    staying = pltpu.make_async_copy(part_ref.at[slot_of(0)], out_ref.at[:, here], local_sem)
    staying.start()
    for t in LEAVING[1:-1]:
        arrived(t)
    for t in range(1, UNITS):
        pltpu.make_async_copy(part_ref.at[slot_of(t)], part_ref.at[slot_of(t)], send_sem.at[t]).wait()
    staying.wait()


def spread(plans, queries, kv, sums):
    dma = pltpu.SemaphoreType.DMA
    vmem = pl.BlockSpec(memory_space=pltpu.VMEM)
    return pl.pallas_call(
        spread_kernel,
        name="spread",
        out_shape=pltpu.VMEM((BLOCK, HEADS * HEAD_DIM), BF16),
        in_specs=[pl.BlockSpec(memory_space=pltpu.SMEM)] + [vmem] * 5,
        out_specs=vmem,
        scratch_shapes=[pltpu.VMEM((UNITS, BLOCK, WIDE), BF16)]
        + [pltpu.VMEM((GROUP * BLOCK, 128), jnp.float32)] * 3
        + [dma, dma((UNITS,)), dma((UNITS,))],
        compiler_params=pltpu.CompilerParams(
            vmem_limit_bytes=ATTEND_MIB * 2**20, collective_id=1, has_side_effects=True
        ),
    )(plans, queries, kv, *sums)


def shards(
    queries, prefix_keys, prefix_values, suffix_keys, suffix_values, layout_pre, layout_suf, lengths
):
    kv, q_all, plans, *begun = gather(
        queries[0], prefix_keys, prefix_values, suffix_keys[0], suffix_values[0],
        plan(layout_pre[0], layout_suf[0], lengths),
    )
    plans = plans[:, 0]
    sums = attend(plans, q_all, kv, begun)
    return spread(plans, q_all, kv, sums)[None]


def solution(mesh):
    return jax.shard_map(
        shards,
        mesh=mesh,
        in_specs=(
            P("samp", "seq", None),
            P("seq", None),
            P("seq", None),
            P("samp", "seq", None),
            P("samp", "seq", None),
            P("samp", "seq", None),
            P("samp", "seq", None),
            P("samp"),
        ),
        out_specs=P("samp", "seq", None),
        check_vma=False,
    )
```

```python
import math

import jax
import jax.numpy as jnp
from jax import lax
from jax.experimental import pallas as pl
from jax.experimental.pallas import tpu as pltpu
from jax.sharding import PartitionSpec as P

HEADS = 40
KV_HEADS = 8
HEAD_DIM = 128
BLOCK = 128
GROUP = HEADS // KV_HEADS
WIDE = GROUP * HEAD_DIM
CHUNK = 4
EARLY = 1
BEFORE = 3
ATTEND_MIB = 24
PLANE = (4, 1, 5, 2, 6, 3, 7)
LEAVING = (5, 3, 7, 4, 1, 2, 6, 0)
FIRST = CHUNK * EARLY
UNITS = 8
MASKED = -1e30
MESH = pl.DeviceIdType.MESH
BF16 = jnp.bfloat16

STEPS = tuple((t // 2, t % 2) for t in range(UNITS))


class Place:
    def __init__(self):
        seq = lax.axis_index("seq")
        samp = lax.axis_index("samp")
        self.z = seq // 8
        self.y = lax.rem(seq // 2, 4)
        self.x = lax.rem(seq, 2)
        self.half = samp // 2
        self.core = lax.rem(samp, 2)
        self.member = self.z * 2 + self.x

    def device(self, dz=0, dy=0, dx=0, dc=0):
        z = lax.rem(self.z + dz, 4)
        y = lax.rem(self.y + dy, 4)
        x = lax.rem(self.x + dx, 2)
        core = lax.rem(self.core + dc, 2)
        return ((z * 4 + y) * 2 + x, self.half * 2 + core)

    def member_at(self, dz, dx):
        return lax.rem(self.z + dz, 4) * 2 + lax.rem(self.x + dx, 2)


def columns(member, width):
    return pl.ds(pl.multiple_of(member * width, width), width)


def meet(partners):
    barrier = pltpu.get_barrier_semaphore()
    for partner in partners:
        pl.semaphore_signal(barrier, inc=1, device_id=partner, device_id_type=MESH)
    pl.semaphore_wait(barrier, len(partners))


def plane_partners(at):
    partners = []
    for dz, dx in STEPS[1:]:
        partners.append(at.device(dz=dz, dx=dx))
        if dx:
            partners.append(at.device(dz=dz, dx=dx, dc=1))
    return partners


def place_of(j):
    return ((j // 2) % 4) * 8 + (j // 8) * 2 + j % 2


def plan_kernel(pre_ref, suf_ref, lengths_ref, plan_ref):
    at = Place()
    block = (at.z * 4 + at.y) * 2 + at.x
    for j in range(FIRST):
        plan_ref[0, j] = 0
    end = jnp.int32(0)
    for j in range(32):
        plan_ref[0, end] = place_of(j)
        end = end + jnp.where(pre_ref[0, j] > 0, 1, 0)
    plan_ref[0, 120] = end
    end = jnp.maximum(end, FIRST)
    for j in range(32):
        plan_ref[0, end] = 32 + place_of(j)
        end = end + jnp.where((suf_ref[0, j] > 0) & (j < block), 1, 0)
    plan_ref[0, 121] = end - FIRST
    plan_ref[0, 122] = jnp.where(block < lengths_ref[0], 1, 0)


def plan(layout_pre, layout_suf, lengths):
    smem = pl.BlockSpec(memory_space=pltpu.SMEM)
    return pl.pallas_call(
        plan_kernel,
        name="plan",
        out_shape=jax.ShapeDtypeStruct((1, 128), jnp.int32),
        in_specs=[smem] * 3,
        out_specs=smem,
    )(layout_pre, layout_suf, lengths)


FACTOR = math.log2(math.e) / math.sqrt(HEAD_DIM)


def stacked(q_ref, slot):
    return jnp.concatenate([q_ref[slot, :, g * HEAD_DIM:(g + 1) * HEAD_DIM] for g in range(GROUP)], axis=0)


def spread_over(column):
    return jnp.broadcast_to(column, (column.shape[0], 128))


def scores_of(q, key_blocks):
    k = jnp.concatenate(key_blocks, axis=0)
    return lax.dot_general(q, k, (((1,), (1,)), ((), ())), preferred_element_type=jnp.float32)


def take_in(s, value_blocks, before, after):
    (m_old, l_old, acc_old), (m_ref, l_ref, acc_ref) = before, after
    old = m_old[...]
    new = jnp.maximum(old, spread_over(jnp.max(s, axis=1, keepdims=True)))
    scale = jnp.exp2((old - new) * FACTOR)
    weights = jnp.exp2((s - jnp.concatenate([new] * CHUNK, axis=1)) * FACTOR)
    m_ref[...] = new
    l_ref[...] = l_old[...] * scale + spread_over(jnp.sum(weights, axis=1, keepdims=True))
    acc_ref[...] = acc_old[...] * scale + lax.dot_general(
        weights.astype(BF16), jnp.concatenate(value_blocks, axis=0), (((1,), (0,)), ((), ())),
        preferred_element_type=jnp.float32,
    )


def gather_kernel(
    q_ref, pk_ref, pv_ref, sk_ref, sv_ref, lay_ref, kvs_ref, qall_ref, layall_ref, m_ref, l_ref, acc_ref,
    kvp_ref, plans, local_sem,
    a_suf_s, a_suf_r, a_pre_s, a_pre_r, a_q_s, a_q_r, a_lay_s, a_lay_r,
    y_suf_s, y_suf_r, y_pre_s, y_pre_r,
    c_suf_s, c_suf_r, c_pre_s, c_pre_r,
):
    at = Place()
    half_rows = BLOCK // 2
    mine = pl.ds(pl.multiple_of(at.core * half_rows, half_rows), half_rows)
    other = pl.ds(pl.multiple_of((1 - at.core) * half_rows, half_rows), half_rows)
    sides = (at.device(dy=1), at.device(dy=3))
    twin = at.device(dc=1)
    meet(plane_partners(at) + [*sides, twin])

    def send(src, dst, send_sem, recv_sem, device):
        pltpu.make_async_remote_copy(
            src_ref=src, dst_ref=dst, send_sem=send_sem, recv_sem=recv_sem, device_id=device, device_id_type=MESH
        ).start()

    def suf_at(dy, member):
        return 32 + lax.rem(at.y + dy, 4) * 8 + member

    def pre_at(dy, member):
        return lax.rem(at.y + dy, 4) * 8 + member

    own_columns = columns(at.member, HEAD_DIM)
    own_k, own_v = sk_ref.at[:, own_columns], sv_ref.at[:, own_columns]
    own_pk, own_pv = pk_ref.at[mine, own_columns], pv_ref.at[mine, own_columns]
    suf_here, pre_here = suf_at(0, at.member), pre_at(0, at.member)

    def own_blocks(k, v, ref, places, sems, recvs, device, rows=None):
        for which, part in ((0, k), (1, v)):
            dst = ref.at[places, which] if rows is None else ref.at[places, which, rows]
            send(part, dst, sems, recvs, device)

    for t in PLANE:
        dz, dx = STEPS[t]
        there = columns(at.member_at(dz, dx), HEAD_DIM)
        own_blocks(pk_ref.at[mine, there], pv_ref.at[mine, there], kvp_ref, pre_here, a_pre_s.at[t], a_pre_r.at[t],
                   at.device(dz=dz, dx=dx), mine)
    for way, device in enumerate(sides):
        own_blocks(own_pk, own_pv, kvp_ref, pre_here, y_pre_s.at[way, 0], y_pre_r.at[way, 0], device, mine)
    own_blocks(own_pk, own_pv, kvp_ref, pre_here, c_pre_s.at[0, 0], c_pre_r.at[0, 0], twin, mine)
    for t in PLANE:
        dz, dx = STEPS[t]
        there = columns(at.member_at(dz, dx), HEAD_DIM)
        own_blocks(sk_ref.at[:, there], sv_ref.at[:, there], kvs_ref, suf_here, a_suf_s.at[t], a_suf_r.at[t],
                   at.device(dz=dz, dx=dx))
    for t in range(1, UNITS):
        dz, dx = STEPS[t]
        device = at.device(dz=dz, dx=dx, dc=dx)
        there = columns(at.member_at(dz, dx), WIDE)
        send(lay_ref, layall_ref.at[at.z * 2 + dx], a_lay_s.at[t], a_lay_r.at[t], device)
        send(q_ref.at[:, there], qall_ref.at[at.z * 2 + dx], a_q_s.at[t], a_q_r.at[t], device)

    q_columns = columns(at.member, WIDE)
    staying = [
        pltpu.make_async_copy(own_k, kvs_ref.at[suf_here, 0], local_sem.at[0]),
        pltpu.make_async_copy(own_v, kvs_ref.at[suf_here, 1], local_sem.at[1]),
        pltpu.make_async_copy(own_pk, kvp_ref.at[pre_here, 0, mine], local_sem.at[2]),
        pltpu.make_async_copy(own_pv, kvp_ref.at[pre_here, 1, mine], local_sem.at[3]),
        pltpu.make_async_copy(q_ref.at[:, q_columns], qall_ref.at[at.z * 2], local_sem.at[4]),
        pltpu.make_async_copy(lay_ref, layall_ref.at[at.z * 2], local_sem.at[5]),
    ]
    for copy in staying:
        copy.start()

    def arrived(block, sem):
        pltpu.make_async_copy(block, block, sem).wait()

    def source(t):
        return at.member_at(4 - t // 2, t % 2)

    def suf_block(dy, t):
        return kvs_ref.at[suf_at(dy, source(t))]

    def pre_block(dy, t, rows=mine):
        return kvp_ref.at[pre_at(dy, source(t)), :, rows]

    def suf_to_twin(dy, t):
        place = suf_at(dy, source(t))
        send(kvs_ref.at[place], kvs_ref.at[place + 32], c_suf_s.at[dy, t], c_suf_r.at[dy, t], twin)

    def pre_to_twin(dy, t):
        block = pre_block(dy, t)
        send(block, block, c_pre_s.at[dy, t], c_pre_r.at[dy, t], twin)

    def side(way):
        return at.device(dy=1 + 2 * way)

    def pre_from_side(way, t, relays):
        block = pre_block(3 - 2 * way, t)
        arrived(block, y_pre_r.at[way, t])
        if relays:
            send(block, block, y_pre_s.at[2, t], y_pre_r.at[2, t], side(way))
        pre_to_twin(3 - 2 * way, t)

    def suf_from_side(way, t, relays):
        block = suf_block(3 - 2 * way, t)
        arrived(block, y_suf_r.at[way, t])
        if relays:
            send(block, block, y_suf_s.at[2, t], y_suf_r.at[2, t], side(way))
        suf_to_twin(3 - 2 * way, t)

    def both(count=4):
        return [(way, 4 * way + i) for i in range(count) for way in range(2)]

    def along(way, t, block, send_sem, recv_sem):
        if t:
            send(block, block, send_sem.at[way, t], recv_sem.at[way, t], sides[way])

    for way, t in both():
        if t:
            arrived(pre_block(0, t), a_pre_r.at[t])
        along(way, t, pre_block(0, t), y_pre_s, y_pre_r)
    for way, t in both():
        along(1 - way, t, pre_block(0, t), y_pre_s, y_pre_r)
    for way, t in both():
        pre_from_side(way, t, True)
    own_blocks(own_k, own_v, kvs_ref, suf_here, y_suf_s.at[0, 0], y_suf_r.at[0, 0], sides[0])
    for way, t in both():
        if t:
            arrived(suf_block(0, t), a_suf_r.at[t])
        along(way, t, suf_block(0, t), y_suf_s, y_suf_r)
    own_blocks(own_k, own_v, kvs_ref, suf_here, y_suf_s.at[1, 0], y_suf_r.at[1, 0], sides[1])
    for way, t in both():
        along(1 - way, t, suf_block(0, t), y_suf_s, y_suf_r)
    for t in range(1, UNITS):
        pre_to_twin(0, t)
    own_blocks(own_k, own_v, kvs_ref, suf_here + 32, c_suf_s.at[0, 0], c_suf_r.at[0, 0], twin)
    for t in range(1, UNITS):
        suf_to_twin(0, t)
    for way, t in both():
        pre_from_side(1 - way, t, False)
    for t in range(UNITS):
        arrived(pre_block(2, t), y_pre_r.at[2, t])
        pre_to_twin(2, t)
    for t in range(UNITS):
        for dy in range(4):
            arrived(pre_block(dy, t, other), c_pre_r.at[dy, t])

    def slot_of(t):
        return lax.rem(at.z + 4 - t // 2, 4) * 2 + t % 2

    for t in range(1, UNITS):
        arrived(layall_ref.at[slot_of(t)], a_lay_r.at[t])
    for copy in staying:
        copy.wait()
    copy = pltpu.make_async_copy(layall_ref, plans, local_sem.at[6])
    copy.start()
    copy.wait()

    keep = pltpu.make_async_copy(kvp_ref, kvs_ref.at[pl.ds(0, 32)], local_sem.at[7])
    keep.start()

    def first_blocks(t):
        slot = slot_of(t)
        q = stacked(qall_ref, slot)
        m, l, acc = m_ref.at[slot], l_ref.at[slot], acc_ref.at[slot]
        m[...] = jnp.full((GROUP * BLOCK, 128), MASKED, jnp.float32)
        l[...] = jnp.zeros((GROUP * BLOCK, 128), jnp.float32)
        acc[...] = jnp.zeros((GROUP * BLOCK, HEAD_DIM), jnp.float32)
        valid = plans[slot, 0, 120]

        @pl.loop(0, EARLY)
        def _(step):
            places = [plans[slot, 0, step * CHUNK + i] for i in range(CHUNK)]
            s = scores_of(q, [kvp_ref[p, 0] for p in places])
            col = lax.broadcasted_iota(jnp.int32, (1, CHUNK * BLOCK), 1)
            s = s + jnp.where(col < (valid - step * CHUNK) * BLOCK, 0.0, MASKED)
            take_in(s, [kvp_ref[p, 1] for p in places], (m, l, acc), (m, l, acc))

    @pl.loop(0, BEFORE)
    def _(t):
        @pl.when(t > 0)
        def _():
            arrived(qall_ref.at[slot_of(t)], a_q_r.at[t])
        first_blocks(t)

    for way, t in both():
        suf_from_side(way, t, True)

    @pl.loop(BEFORE, UNITS)
    def _(t):
        arrived(qall_ref.at[slot_of(t)], a_q_r.at[t])
        first_blocks(t)

    for way, t in both():
        suf_from_side(1 - way, t, False)
    for t in range(UNITS):
        arrived(suf_block(2, t), y_suf_r.at[2, t])
        suf_to_twin(2, t)

    keep.wait()
    for t in range(UNITS):
        for dy in range(4):
            arrived(kvs_ref.at[suf_at(dy, source(t)) + 32], c_suf_r.at[dy, t])
    suf, pre = suf_block(0, 0), pre_block(0, 0)
    for t in range(UNITS):
        if t:
            arrived(suf, a_suf_s.at[t])
            arrived(pre, a_pre_s.at[t])
            arrived(qall_ref.at[at.z * 2], a_q_s.at[t])
            arrived(layall_ref.at[at.z * 2], a_lay_s.at[t])
        for way in range(3):
            arrived(suf, y_suf_s.at[way, t])
            arrived(pre, y_pre_s.at[way, t])
        for dy in range(4):
            arrived(suf, c_suf_s.at[dy, t])
            arrived(pre, c_pre_s.at[dy, t])


def gather(queries, prefix_keys, prefix_values, suffix_keys, suffix_values, layout):
    dma = pltpu.SemaphoreType.DMA
    anywhere = pl.BlockSpec(memory_space=pl.ANY)
    return pl.pallas_call(
        gather_kernel,
        name="gather",
        out_shape=(
            pltpu.VMEM((96, 2, BLOCK, HEAD_DIM), BF16),
            pltpu.VMEM((UNITS, BLOCK, WIDE), BF16),
            pltpu.VMEM((UNITS, 1, 128), jnp.int32),
            pltpu.VMEM((UNITS, GROUP * BLOCK, 128), jnp.float32),
            pltpu.VMEM((UNITS, GROUP * BLOCK, 128), jnp.float32),
            pltpu.VMEM((UNITS, GROUP * BLOCK, HEAD_DIM), jnp.float32),
        ),
        in_specs=[pl.BlockSpec(memory_space=pltpu.HBM)] * 6,
        out_specs=(pl.BlockSpec(memory_space=pltpu.VMEM),) * 6,
        scratch_shapes=[
            pltpu.VMEM((32, 2, BLOCK, HEAD_DIM), BF16),
            pltpu.SMEM((UNITS, 1, 128), jnp.int32),
            dma((8,)),
        ]
        + [dma((UNITS,))] * 8
        + [dma((3, UNITS))] * 4
        + [dma((4, UNITS))] * 4,
        compiler_params=pltpu.CompilerParams(vmem_limit_bytes=40 * 2**20, collective_id=0, has_side_effects=True),
    )(queries, prefix_keys, prefix_values, suffix_keys, suffix_values, layout)


def entry_of(plan_ref, slot, at_entry):
    place = plan_ref[slot, FIRST + at_entry]
    return jnp.where(place < 32, place, place + 32 * lax.rem(slot, 2))


def attend_kernel(plan_ref, q_ref, kv_ref, m_in, l_in, acc_in, m_out, l_out, acc_out):
    unit = pl.program_id(0)

    @pl.when(plan_ref[unit, 122] > 0)
    def _():
        count = plan_ref[unit, 121]
        spare = lax.rem(count, CHUNK)
        q = stacked(q_ref, unit)
        sums = m_out.at[unit], l_out.at[unit], acc_out.at[unit]
        for before, after in zip((m_in, l_in, acc_in), sums):
            after[...] = before[unit]

        @pl.loop(0, count // CHUNK)
        def _(step):
            places = [entry_of(plan_ref, unit, spare + step * CHUNK + s) for s in range(CHUNK)]
            s = scores_of(q, [kv_ref[p, 0] for p in places])
            take_in(s, [kv_ref[p, 1] for p in places], sums, sums)


def attend(plans, queries, kv, begun):
    vmem = pl.BlockSpec(memory_space=pltpu.VMEM)
    return pl.pallas_call(
        attend_kernel,
        name="attend",
        grid=(UNITS,),
        out_shape=(pltpu.VMEM((UNITS, GROUP * BLOCK, 128), jnp.float32),) * 3,
        in_specs=[pl.BlockSpec(memory_space=pltpu.SMEM)] + [vmem] * 5,
        out_specs=(vmem,) * 3,
        compiler_params=pltpu.CompilerParams(
            vmem_limit_bytes=ATTEND_MIB * 2**20, dimension_semantics=("arbitrary",)
        ),
    )(plans, queries, kv, *begun)


def spread_kernel(
    plan_ref, q_ref, kv_ref, m_ref, l_ref, acc_ref, out_ref, part_ref, m_end, l_end, acc_end, local_sem, send_sem, recv_sem
):
    at = Place()
    barrier = pltpu.get_barrier_semaphore()
    for dz, dx in STEPS[1:]:
        pl.semaphore_signal(barrier, inc=1, device_id=at.device(dz=dz, dx=dx, dc=dx), device_id_type=MESH)
    here = columns(at.member, WIDE)

    def slot_of(t):
        return lax.rem(at.z + t // 2, 4) * 2 + t % 2

    def last_blocks(t):
        slot = slot_of(t)
        z, x = lax.rem(at.z + t // 2, 4), lax.rem(at.x + t % 2, 2)
        diagonal = 32 + 32 * (t % 2) + at.y * 8 + z * 2 + x
        spare = lax.rem(plan_ref[slot, 121], CHUNK)
        places = [diagonal]
        for s in range(CHUNK - 1):
            places.append(jnp.where(s < spare, entry_of(plan_ref, slot, s), diagonal))
        s = scores_of(stacked(q_ref, slot), [kv_ref[p, 0] for p in places])
        row = lax.broadcasted_iota(jnp.int32, s.shape, 0) % BLOCK
        col = lax.broadcasted_iota(jnp.int32, s.shape, 1)
        last = jnp.where(col < BLOCK, row, (spare + 1) * BLOCK - 1)
        take_in(
            jnp.where(col <= last, s, MASKED), [kv_ref[p, 1] for p in places],
            (m_ref.at[slot], l_ref.at[slot], acc_ref.at[slot]), (m_end, l_end, acc_end),
        )
        out = jnp.where(plan_ref[slot, 122] > 0, acc_end[...] / l_end[...], 0.0).astype(BF16)
        for g in range(GROUP):
            part_ref[slot, :, g * HEAD_DIM:(g + 1) * HEAD_DIM] = out[g * BLOCK:(g + 1) * BLOCK]

    for i, t in enumerate(LEAVING):
        last_blocks(t)
        if i == 0:
            pl.semaphore_wait(barrier, UNITS - 1)
            continue
        gone = LEAVING[i - 1]
        pltpu.make_async_remote_copy(
            src_ref=part_ref.at[slot_of(gone)],
            dst_ref=out_ref.at[:, here],
            send_sem=send_sem.at[gone],
            recv_sem=recv_sem.at[gone],
            device_id=at.device(dz=gone // 2, dx=gone % 2, dc=gone % 2),
            device_id_type=MESH,
        ).start()

    def arrived(t):
        there = out_ref.at[:, columns(at.member_at(4 - t // 2, t % 2), WIDE)]
        pltpu.make_async_copy(there, there, recv_sem.at[t]).wait()

    arrived(LEAVING[0])
    staying = pltpu.make_async_copy(part_ref.at[slot_of(0)], out_ref.at[:, here], local_sem)
    staying.start()
    for t in LEAVING[1:-1]:
        arrived(t)
    for t in range(1, UNITS):
        pltpu.make_async_copy(part_ref.at[slot_of(t)], part_ref.at[slot_of(t)], send_sem.at[t]).wait()
    staying.wait()


def spread(plans, queries, kv, sums):
    dma = pltpu.SemaphoreType.DMA
    vmem = pl.BlockSpec(memory_space=pltpu.VMEM)
    return pl.pallas_call(
        spread_kernel,
        name="spread",
        out_shape=pltpu.VMEM((BLOCK, HEADS * HEAD_DIM), BF16),
        in_specs=[pl.BlockSpec(memory_space=pltpu.SMEM)] + [vmem] * 5,
        out_specs=vmem,
        scratch_shapes=[pltpu.VMEM((UNITS, BLOCK, WIDE), BF16)]
        + [pltpu.VMEM((GROUP * BLOCK, 128), jnp.float32)] * 3
        + [dma, dma((UNITS,)), dma((UNITS,))],
        compiler_params=pltpu.CompilerParams(
            vmem_limit_bytes=ATTEND_MIB * 2**20, collective_id=1, has_side_effects=True
        ),
    )(plans, queries, kv, *sums)


def shards(
    queries, prefix_keys, prefix_values, suffix_keys, suffix_values, layout_pre, layout_suf, lengths
):
    kv, q_all, plans, *begun = gather(
        queries[0], prefix_keys, prefix_values, suffix_keys[0], suffix_values[0],
        plan(layout_pre[0], layout_suf[0], lengths),
    )
    plans = plans[:, 0]
    sums = attend(plans, q_all, kv, begun)
    return spread(plans, q_all, kv, sums)[None]


def solution(mesh):
    return jax.shard_map(
        shards,
        mesh=mesh,
        in_specs=(
            P("samp", "seq", None),
            P("seq", None),
            P("seq", None),
            P("samp", "seq", None),
            P("samp", "seq", None),
            P("samp", "seq", None),
            P("samp", "seq", None),
            P("samp"),
        ),
        out_specs=P("samp", "seq", None),
        check_vma=False,
    )
```
